32 devices in a mesh: shard: 2 (over x), heads: 4 (over z), tensor: 4 (over y, core).
Axes of the slice: x: 2, y: 2, z: 4, core: 2. Of those that a mesh axis runs over, the one named last changes fastest.
Arguments:
- patch_pixels: bfloat16 [64, 196, 768], P(('shard', 'heads')), may hold values from -6 to 6
- keep_index: int32 [64, 49], P(('shard', 'heads')), may hold values from 0 to 195, as said below
- restore_index: int32 [64, 196], P(('shard', 'heads')), may hold values from 0 to 195, as said below
- masked: int32 [64, 196], P(('shard', 'heads')), may hold values from 0 to 1, as said below
- encoder_mats: float32 [768, 4352], P(('shard', 'heads')), may hold values from -0.21875 to 0.21875
- encoder_mats_first: float32 [768, 4352], P(('shard', 'heads'))
- encoder_mats_second: float32 [768, 4352], P(('shard', 'heads')), as said below
- decoder_mats: float32 [512, 2816], P(('shard', 'heads')), may hold values from -0.25 to 0.25
- decoder_mats_first: float32 [512, 2816], P(('shard', 'heads'))
- decoder_mats_second: float32 [512, 2816], P(('shard', 'heads')), as said below
- encoder_feed: float32 [2, 768, 3072], P(None, ('shard', 'heads'), 'tensor'), may hold values from -0.15625 to 0.15625
- encoder_feed_first: float32 [2, 768, 3072], P(None, ('shard', 'heads'), 'tensor')
- encoder_feed_second: float32 [2, 768, 3072], P(None, ('shard', 'heads'), 'tensor'), as said below
- decoder_feed: float32 [2, 512, 2048], P(None, ('shard', 'heads'), 'tensor'), may hold values from -0.1875 to 0.1875
- decoder_feed_first: float32 [2, 512, 2048], P(None, ('shard', 'heads'), 'tensor')
- decoder_feed_second: float32 [2, 512, 2048], P(None, ('shard', 'heads'), 'tensor'), as said below
- encoder_norms: float32 [6, 768], P(None, ('shard', 'heads')), as said below
- encoder_norms_first: float32 [6, 768], P(None, ('shard', 'heads'))
- encoder_norms_second: float32 [6, 768], P(None, ('shard', 'heads')), as said below
- decoder_norms: float32 [7, 512], P(None, ('shard', 'heads')), as said below
- decoder_norms_first: float32 [7, 512], P(None, ('shard', 'heads'))
- decoder_norms_second: float32 [7, 512], P(None, ('shard', 'heads')), as said below
Outputs:
- masked_loss: float32 [], replicated
- gradient_norm: float32 [], replicated
- encoder_mats_new: float32 [768, 4352], P(('shard', 'heads'))
- encoder_mats_first_new: float32 [768, 4352], P(('shard', 'heads'))
- encoder_mats_second_new: float32 [768, 4352], P(('shard', 'heads'))
- decoder_mats_new: float32 [512, 2816], P(('shard', 'heads'))
- decoder_mats_first_new: float32 [512, 2816], P(('shard', 'heads'))
- decoder_mats_second_new: float32 [512, 2816], P(('shard', 'heads'))
- encoder_feed_new: float32 [2, 768, 3072], P(None, ('shard', 'heads'), 'tensor')
- encoder_feed_first_new: float32 [2, 768, 3072], P(None, ('shard', 'heads'), 'tensor')
- encoder_feed_second_new: float32 [2, 768, 3072], P(None, ('shard', 'heads'), 'tensor')
- decoder_feed_new: float32 [2, 512, 2048], P(None, ('shard', 'heads'), 'tensor')
- decoder_feed_first_new: float32 [2, 512, 2048], P(None, ('shard', 'heads'), 'tensor')
- decoder_feed_second_new: float32 [2, 512, 2048], P(None, ('shard', 'heads'), 'tensor')
- encoder_norms_new: float32 [6, 768], P(None, ('shard', 'heads'))
- encoder_norms_first_new: float32 [6, 768], P(None, ('shard', 'heads'))
- encoder_norms_second_new: float32 [6, 768], P(None, ('shard', 'heads'))
- decoder_norms_new: float32 [7, 512], P(None, ('shard', 'heads'))
- decoder_norms_first_new: float32 [7, 512], P(None, ('shard', 'heads'))
- decoder_norms_second_new: float32 [7, 512], P(None, ('shard', 'heads'))
The draws below stay inside these ranges and needn't reach their ends.
Inputs may be any that keep to these rules, and one draw needn't show every extreme that they name: `keep_index`: each row holds 49 different patch numbers, the first 49 of that image's shuffle. Each row is a permutation, the inverse of the image's shuffle: restore_index[i, keep_index[i, j]] = j. masked[i, p] = 1 exactly where restore_index[i, p] >= 49. `encoder_norms`: rows 0, 2, 4 are gains, rows 1, 3, 5 offsets. `decoder_norms`: rows 0, 2, 4 are gains, rows 1, 3, 5 offsets, row 6 the mask token. `encoder_mats_second`: every entry is positive. `decoder_mats_second`: every entry is positive. `encoder_feed_second`: every entry is positive. `decoder_feed_second`: every entry is positive. `encoder_norms_second`: every entry is positive. `decoder_norms_second`: every entry is positive.
All inputs are finite; a program needn't handle non-finite values.
Results may differ from the reference program's by a relative error of at most 0.0096.
Values may be sent and summed in bfloat16 or wider, within the bound.
No kernel may reach another device: no remote copies, remote signals or barrier semaphores. Data moves between devices by JAX's collectives and lax.ppermute only.
A program may use at most 192 MiB of HBM per device.

```python
import math
from functools import partial
import jax
import jax.numpy as jnp
from jax import lax

PATCH_DIM = 768
D_ENC = 768
HEADS_E = 12
FF_E = 3072
D_DEC = 512
HEADS_D = 16
FF_D = 2048
PATCHES = 196
KEEP = 49
STEP = 5
IMAGES = 64
ENC_COLS = 4352
DEC_COLS = 2816
PARAMS = 11608064


clip_limit = 0.01


def shuffled(key):
    keys = jax.random.split(jax.random.fold_in(key, 11), IMAGES)
    return jax.vmap(lambda member: jax.random.permutation(member, PATCHES))(keys).astype(jnp.int32)


def draw_keep_index(key, part):
    return shuffled(key)[:, :KEEP]


def draw_restore_index(key, part):
    return jnp.argsort(shuffled(key), axis=1).astype(jnp.int32)


def draw_masked(key, part):
    return (draw_restore_index(key, part) >= KEEP).astype(jnp.int32)


def grad_scale(factor):
    return factor * clip_limit / math.sqrt(PARAMS)


def first_moment(key, salt, shape, factor):
    own_key = jax.random.fold_in(jax.random.fold_in(key, 101), salt)
    return jax.random.normal(jax.random.fold_in(own_key, 3), shape, jnp.float32) * (grad_scale(factor) / 9.0)


def second_moment(key, salt, shape, factor):
    own_key = jax.random.fold_in(jax.random.fold_in(key, 202), salt)
    spread = jnp.exp(jax.random.uniform(jax.random.fold_in(own_key, 5), shape, jnp.float32, 0.0, math.log(4.0)))
    return spread * (grad_scale(factor) ** 2 / 999.0)


def norm_table(key, salt, count, features):
    own_key = jax.random.fold_in(jax.random.fold_in(key, 303), salt)
    rows = jnp.arange(count)[:, None]
    gains = jnp.clip(1.0 + 0.15 * jax.random.normal(jax.random.fold_in(own_key, 1), (count, features), jnp.float32), 0.5, 1.5)
    shifts = 0.3 * jax.random.normal(jax.random.fold_in(own_key, 2), (count, features), jnp.float32)
    token = jax.random.normal(jax.random.fold_in(own_key, 4), (count, features), jnp.float32)
    return jnp.where(rows == 6, token, jnp.where(rows % 2 == 0, gains, shifts))


def draw_encoder_norms(key, part):
    return norm_table(key, 1, 6, D_ENC)


def draw_decoder_norms(key, part):
    return norm_table(key, 2, 7, D_DEC)


def draw_encoder_mats_first(key, part):
    return first_moment(key, 1, (D_ENC, ENC_COLS), 1.0)


def draw_encoder_mats_second(key, part):
    return second_moment(key, 1, (D_ENC, ENC_COLS), 1.0)


def draw_decoder_mats_first(key, part):
    return first_moment(key, 2, (D_DEC, DEC_COLS), 1.0)


def draw_decoder_mats_second(key, part):
    return second_moment(key, 2, (D_DEC, DEC_COLS), 1.0)


def draw_encoder_feed_first(key, part):
    return first_moment(key, 3, (2, D_ENC, FF_E), 1.0)


def draw_encoder_feed_second(key, part):
    return second_moment(key, 3, (2, D_ENC, FF_E), 1.0)


def draw_decoder_feed_first(key, part):
    return first_moment(key, 4, (2, D_DEC, FF_D), 1.0)


def draw_decoder_feed_second(key, part):
    return second_moment(key, 4, (2, D_DEC, FF_D), 1.0)


def draw_encoder_norms_first(key, part):
    return first_moment(key, 5, (6, D_ENC), 1.5)


def draw_encoder_norms_second(key, part):
    return second_moment(key, 5, (6, D_ENC), 1.5)


def draw_decoder_norms_first(key, part):
    return first_moment(key, 6, (7, D_DEC), 4.0)


def draw_decoder_norms_second(key, part):
    return second_moment(key, 6, (7, D_DEC), 4.0)


def block_scale(key, extent, shards, smallest, high):
    factor_of, own = 1.0, jax.random.fold_in(key, 6)
    for position, blocks in shards:
        steps = jnp.exp(jax.random.uniform(jax.random.fold_in(own, position), (blocks,), jnp.float32, smallest / len(shards), high / len(shards)))
        factor_of = factor_of * jnp.repeat(steps, extent[position] // blocks).reshape([-1 if axis == position else 1 for axis in range(len(extent))])
    return factor_of


def scatter_about(key, extent, scale, bound, shards=(), kind=jnp.bfloat16):
    values = scale * jax.random.normal(key, extent, jnp.float32)
    if shards:
        values = values * block_scale(key, extent, shards, -0.22, 0.18)
    return jnp.clip(values, -bound, bound).astype(kind)


def setup_inputs(seed: int = 0) -> dict:
    key_list = jax.random.split(jax.random.key(seed), 23)
    patch_pixels = scatter_about(key_list[0], (IMAGES, PATCHES, PATCH_DIM), 1.0, 6.0, ((0, 8),))
    keep_index = draw_keep_index(jax.random.fold_in(key_list[22], 71), 0)
    restore_index = draw_restore_index(jax.random.fold_in(key_list[22], 71), 0)
    masked = draw_masked(jax.random.fold_in(key_list[22], 71), 0)
    encoder_mats = scatter_about(key_list[4], (D_ENC, ENC_COLS), D_ENC ** -0.5, 0.21875, ((0, 8),), jnp.float32)
    encoder_mats_first = draw_encoder_mats_first(jax.random.fold_in(key_list[22], 71), 0)
    encoder_mats_second = draw_encoder_mats_second(jax.random.fold_in(key_list[22], 71), 0)
    decoder_mats = scatter_about(key_list[7], (D_DEC, DEC_COLS), D_DEC ** -0.5, 0.25, ((0, 8),), jnp.float32)
    decoder_mats_first = draw_decoder_mats_first(jax.random.fold_in(key_list[22], 71), 0)
    decoder_mats_second = draw_decoder_mats_second(jax.random.fold_in(key_list[22], 71), 0)
    encoder_feed = scatter_about(key_list[10], (2, D_ENC, FF_E), (2 * D_ENC) ** -0.5, 0.15625, ((1, 8), (2, 4)), jnp.float32)
    encoder_feed_first = draw_encoder_feed_first(jax.random.fold_in(key_list[22], 71), 0)
    encoder_feed_second = draw_encoder_feed_second(jax.random.fold_in(key_list[22], 71), 0)
    decoder_feed = scatter_about(key_list[13], (2, D_DEC, FF_D), (2 * D_DEC) ** -0.5, 0.1875, ((1, 8), (2, 4)), jnp.float32)
    decoder_feed_first = draw_decoder_feed_first(jax.random.fold_in(key_list[22], 71), 0)
    decoder_feed_second = draw_decoder_feed_second(jax.random.fold_in(key_list[22], 71), 0)
    encoder_norms = draw_encoder_norms(jax.random.fold_in(key_list[22], 71), 0)
    encoder_norms_first = draw_encoder_norms_first(jax.random.fold_in(key_list[22], 71), 0)
    encoder_norms_second = draw_encoder_norms_second(jax.random.fold_in(key_list[22], 71), 0)
    decoder_norms = draw_decoder_norms(jax.random.fold_in(key_list[22], 71), 0)
    decoder_norms_first = draw_decoder_norms_first(jax.random.fold_in(key_list[22], 71), 0)
    decoder_norms_second = draw_decoder_norms_second(jax.random.fold_in(key_list[22], 71), 0)
    return {"patch_pixels": patch_pixels, "keep_index": keep_index, "restore_index": restore_index, "masked": masked, "encoder_mats": encoder_mats, "encoder_mats_first": encoder_mats_first, "encoder_mats_second": encoder_mats_second, "decoder_mats": decoder_mats, "decoder_mats_first": decoder_mats_first, "decoder_mats_second": decoder_mats_second, "encoder_feed": encoder_feed, "encoder_feed_first": encoder_feed_first, "encoder_feed_second": encoder_feed_second, "decoder_feed": decoder_feed, "decoder_feed_first": decoder_feed_first, "decoder_feed_second": decoder_feed_second, "encoder_norms": encoder_norms, "encoder_norms_first": encoder_norms_first, "encoder_norms_second": encoder_norms_second, "decoder_norms": decoder_norms, "decoder_norms_first": decoder_norms_first, "decoder_norms_second": decoder_norms_second}


highest = lax.Precision.HIGHEST
clip_limit = 0.01
beta_one = 0.9
beta_two = 0.999
learn_rate = 0.05
norm_rate = 0.5
decay_rate = 0.05
adam_eps = 1e-08
norm_eps = 1e-06

@jax.custom_vjp
def low(v):
    return lax.optimization_barrier(v.astype(jnp.bfloat16)).astype(jnp.float32)

@jax.custom_vjp
def low_back(v):
    return v

def low_keep(v):
    return (low(v), None)

def low_pass(kept, grad):
    return (grad,)

def back_keep(v):
    return (v, None)

def back_low(kept, grad):
    return (low(grad),)
low.defvjp(low_keep, low_pass)
low_back.defvjp(back_keep, back_low)

def positions(places, features):
    where = jnp.arange(places, dtype=jnp.float32)[:, None]
    column = jnp.arange(features // 2, dtype=jnp.float32)[None, :]
    angles = where * jnp.exp(column * (-2.0 * math.log(10000.0) / features))
    return jnp.concatenate([jnp.sin(angles), jnp.cos(angles)], axis=1)

def layer_norm(rows, gain, shift):
    centered = rows - lax.optimization_barrier(jnp.mean(rows, axis=-1, keepdims=True))
    spread = lax.optimization_barrier(jnp.mean(centered * centered, axis=-1, keepdims=True))
    return centered * lax.rsqrt(spread + norm_eps) * gain + shift

def block_size(leading, length):
    chosen = 1
    for candidate in range(1, max(1, 1024 // length) + 1):
        if leading % candidate == 0:
            chosen = candidate
    return chosen

def attend_block(members, score_scale):
    queries, key_rows, value_rows = members
    scores = low_back(jnp.einsum('blhd,bmhd->bhlm', queries, key_rows, precision=highest) * score_scale)
    shares = jax.nn.softmax(scores, axis=-1)
    return jnp.einsum('bhlm,bmhd->blhd', low(shares), value_rows, precision=highest)

def attend(queries, key_rows, value_rows, score_scale):
    leading, length = (queries.shape[0], queries.shape[1])
    chosen = block_size(leading, length)
    grouped = tuple((member.reshape((leading // chosen, chosen) + member.shape[1:]) for member in (queries, key_rows, value_rows)))
    result = lax.map(jax.checkpoint(partial(attend_block, score_scale=score_scale)), grouped)
    return result.reshape(queries.shape)

def layer(stream, packed_w, out_w, feed, norms, head_count):
    images, length, features = stream.shape
    head_size = features // head_count
    normed = low(layer_norm(stream, norms[0], norms[1])).reshape(images * length, features)
    packed = low(low_back(jnp.dot(normed, packed_w, precision=highest)))
    packed = packed.reshape(images, length, 3, head_count, head_size)
    attended = attend(packed[:, :, 0], packed[:, :, 1], packed[:, :, 2], head_size ** (-0.5))
    attended = low(low_back(attended.reshape(images * length, features)))
    mixed = stream + low_back(jnp.dot(attended, out_w, precision=highest)).reshape(images, length, features)
    second = low(layer_norm(mixed, norms[2], norms[3])).reshape(images * length, features)
    hidden = low(jax.nn.gelu(low_back(jnp.dot(second, feed[0], precision=highest)), approximate=False))
    branch = low_back(jnp.dot(hidden, feed[1].T, precision=highest))
    return mixed + branch.reshape(images, length, features)

def forward(weights, pixels, keep_index, restore_index, masked):
    enc_w, dec_w, enc_feed, dec_feed, enc_norms, dec_norms = weights
    picked = jnp.take_along_axis(pixels, keep_index[:, :, None], axis=1)
    embedded = low_back(jnp.dot(picked.reshape(-1, PATCH_DIM), enc_w[:, :D_ENC], precision=highest))
    stream = embedded.reshape(IMAGES, KEEP, D_ENC) + positions(PATCHES, D_ENC)[keep_index]
    stream = layer(stream, enc_w[:, D_ENC:4 * D_ENC], enc_w[:, 4 * D_ENC:5 * D_ENC], enc_feed, enc_norms, HEADS_E)
    final = low(layer_norm(stream, enc_norms[4], enc_norms[5])).reshape(-1, D_ENC)
    latent = low_back(jnp.dot(final, enc_w[:, 5 * D_ENC:], precision=highest)).reshape(IMAGES, KEEP, D_DEC)
    filler = jnp.broadcast_to(dec_norms[6], (IMAGES, PATCHES - KEEP, D_DEC))
    whole = jnp.concatenate([latent, filler], axis=1)
    stream = jnp.take_along_axis(whole, restore_index[:, :, None], axis=1) + positions(PATCHES, D_DEC)
    stream = layer(stream, dec_w[:, :3 * D_DEC], dec_w[:, 3 * D_DEC:4 * D_DEC], dec_feed, dec_norms, HEADS_D)
    final = low(layer_norm(stream, dec_norms[4], dec_norms[5])).reshape(-1, D_DEC)
    prediction = low_back(jnp.dot(final, dec_w[:, 4 * D_DEC:], precision=highest)).reshape(IMAGES, PATCHES, PATCH_DIM)
    errors = prediction - pixels
    chosen_rows = masked[:, :, None].astype(jnp.float32)
    return jnp.sum(chosen_rows * errors * errors) / (IMAGES * (PATCHES - KEEP) * PATCH_DIM)

def adam_update(weight, first, second, gradient, rate):
    first = beta_one * first + (1.0 - beta_one) * gradient
    second = beta_two * second + (1.0 - beta_two) * gradient * gradient
    fix_one = 1.0 - beta_one ** STEP
    fix_two = 1.0 - beta_two ** STEP
    step_dir = first / fix_one / (jnp.sqrt(second / fix_two) + adam_eps)
    return (weight - rate * (step_dir + decay_rate * weight), first, second)

def reference(patch_pixels, keep_index, restore_index, masked, encoder_mats, encoder_mats_first, encoder_mats_second, decoder_mats, decoder_mats_first, decoder_mats_second, encoder_feed, encoder_feed_first, encoder_feed_second, decoder_feed, decoder_feed_first, decoder_feed_second, encoder_norms, encoder_norms_first, encoder_norms_second, decoder_norms, decoder_norms_first, decoder_norms_second):
    masters = (encoder_mats, decoder_mats, encoder_feed, decoder_feed, encoder_norms, decoder_norms)
    firsts = (encoder_mats_first, decoder_mats_first, encoder_feed_first, decoder_feed_first, encoder_norms_first, decoder_norms_first)
    seconds = (encoder_mats_second, decoder_mats_second, encoder_feed_second, decoder_feed_second, encoder_norms_second, decoder_norms_second)
    rates = (learn_rate, learn_rate, learn_rate, learn_rate, norm_rate, norm_rate)
    pixels = patch_pixels.astype(jnp.float32)

    def loss_of(weights):
        return forward(tuple((low(member) for member in weights)), pixels, keep_index, restore_index, masked)
    loss, pull = jax.vjp(loss_of, masters)
    grads = pull(jnp.ones((), jnp.float32))[0]
    total = sum((jnp.sum(member * member) for member in grads))
    norm = jnp.sqrt(total)
    factor = clip_limit / jnp.maximum(norm, clip_limit)
    results = [loss, norm]
    for weight, first, second, gradient, rate in zip(masters, firsts, seconds, grads, rates):
        results.extend(adam_update(weight, first, second, gradient * factor, rate))
    return (results[0], results[1], results[2], results[3], results[4], results[5], results[6], results[7], results[8], results[9], results[10], results[11], results[12], results[13], results[14], results[15], results[16], results[17], results[18], results[19])
```

```python
from functools import partial
import math

import jax
import jax.numpy as jnp
import numpy as np
from jax import lax
from jax.sharding import Mesh, PartitionSpec as P

HEADS_E = 12
HEADS_D = 16
STEP = 5

clip_limit = 0.01
beta_one = 0.9
beta_two = 0.999
learn_rate = 0.05
norm_rate = 0.5
decay_rate = 0.05
adam_eps = 1e-08
norm_eps = 1e-06

AXES = ("shard", "heads", "pair", "core")
TENSOR = ("pair", "core")
low = jnp.bfloat16


def positions(places, features):
    where = np.arange(places, dtype=np.float32)[:, None]
    column = np.arange(features // 2, dtype=np.float32)[None, :]
    angles = where * np.exp(column * np.float32(-2.0 * math.log(10000.0) / features))
    return np.concatenate([np.sin(angles), np.cos(angles)], axis=1).astype(np.float32)


def layer_norm(rows, gain, shift):
    centered = rows - jnp.mean(rows, axis=-1, keepdims=True)
    spread = jnp.mean(centered * centered, axis=-1, keepdims=True)
    return centered * lax.rsqrt(spread + norm_eps) * gain + shift


def product(left, right):
    return jnp.dot(left, right, preferred_element_type=jnp.float32)


def product_left(left, right):
    return lax.dot_general(
        left, right, (((0,), (0,)), ((), ())), preferred_element_type=jnp.float32
    )


def product_right(left, right):
    return lax.dot_general(
        left, right, (((1,), (1,)), ((), ())), preferred_element_type=jnp.float32
    )


def attend_forward(queries, key_rows, value_rows, score_scale):
    scores = (
        jnp.einsum("blhd,bmhd->bhlm", queries, key_rows, preferred_element_type=jnp.float32)
        * score_scale
    )
    top = jnp.max(scores, axis=-1, keepdims=True)
    powers = jnp.exp(scores - top)
    totals = jnp.sum(powers, axis=-1, keepdims=True)
    shares = (powers / totals).astype(low)
    attended = jnp.einsum("bhlm,bmhd->blhd", shares, value_rows, preferred_element_type=jnp.float32)
    return (attended.astype(low), (top + jnp.log(totals))[..., 0])


def attend_backward(queries, key_rows, value_rows, log_totals, grad_out, score_scale):
    scores = (
        jnp.einsum("blhd,bmhd->bhlm", queries, key_rows, preferred_element_type=jnp.float32)
        * score_scale
    )
    shares = jnp.exp(scores - log_totals[..., None])
    grad_shares = jnp.einsum(
        "blhd,bmhd->bhlm", grad_out, value_rows, preferred_element_type=jnp.float32
    )
    grad_values = jnp.einsum(
        "bhlm,blhd->bmhd", shares.astype(low), grad_out, preferred_element_type=jnp.float32
    )
    inner = jnp.sum(shares * grad_shares, axis=-1, keepdims=True)
    grad_scores = (shares * (grad_shares - inner)).astype(low)
    grad_queries = (
        jnp.einsum("bhlm,bmhd->blhd", grad_scores, key_rows, preferred_element_type=jnp.float32)
        * score_scale
    )
    grad_keys = (
        jnp.einsum("bhlm,blhd->bmhd", grad_scores, queries, preferred_element_type=jnp.float32)
        * score_scale
    )
    return jnp.stack([grad_queries, grad_keys, grad_values], axis=2)


def layer_forward(stream, packed_w, out_w, feed, norms, head_count):
    images, length, features = stream.shape
    head_size = features // head_count
    flat_rows = stream.reshape(images * length, features)
    normed = layer_norm(flat_rows, norms[0], norms[1]).astype(low)
    packed = product(normed, packed_w).astype(low)
    split = packed.reshape(images, length, 3, head_count, head_size)
    attended, log_totals = attend_forward(
        split[:, :, 0], split[:, :, 1], split[:, :, 2], head_size ** (-0.5)
    )
    merged = attended.reshape(images * length, features)
    mixed = flat_rows + product(merged, out_w)
    second = layer_norm(mixed, norms[2], norms[3]).astype(low)
    hidden_pre = [product(second, member) for member in feed[0]]
    hidden = [jax.nn.gelu(member, approximate=False).astype(low) for member in hidden_pre]
    result = sum([product_right(*members) for members in zip(hidden, feed[1])], mixed)
    saved = (flat_rows, normed, split, log_totals, merged, mixed, second, hidden_pre, hidden)
    return (result.reshape(images, length, features), saved)


def layer_backward(gradient, saved, packed_w, out_w, feed, norms, head_count):
    flat_rows, normed, split, log_totals, merged, mixed, second, hidden_pre, hidden = saved
    rows, features = flat_rows.shape
    images, length = split.shape[:2]
    head_size = features // head_count
    grad_branch = gradient.astype(low)
    grad_down = [product_left(grad_branch, member) for member in hidden]
    gelu = partial(jax.nn.gelu, approximate=False)
    grad_pre = [
        jax.vjp(gelu, member)[1](product(grad_branch, weights))[0].astype(low)
        for member, weights in zip(hidden_pre, feed[1])
    ]
    grad_up = [product_left(second, member) for member in grad_pre]
    grad_second = sum(product_right(*members) for members in zip(grad_pre, feed[0]))
    second_pull = jax.vjp(layer_norm, mixed, norms[2], norms[3])[1]
    grad_mixed, gain_two, shift_two = second_pull(grad_second)
    grad_mixed = gradient + grad_mixed
    grad_attn = grad_mixed.astype(low)
    grad_out_w = product_left(merged, grad_attn)
    grad_merged = product_right(grad_attn, out_w).astype(low)
    grad_heads = grad_merged.reshape(images, length, head_count, head_size)
    grad_split = attend_backward(
        split[:, :, 0], split[:, :, 1], split[:, :, 2], log_totals, grad_heads, head_size ** (-0.5)
    ).astype(low)
    grad_packed = grad_split.reshape(rows, 3 * features)
    grad_packed_w = product_left(normed, grad_packed)
    grad_normed = product_right(grad_packed, packed_w)
    first_pull = jax.vjp(layer_norm, flat_rows, norms[0], norms[1])[1]
    grad_rows, gain_one, shift_one = first_pull(grad_normed)
    norm_grads = jnp.stack([gain_one, shift_one, gain_two, shift_two])
    return (
        grad_mixed + grad_rows,
        (grad_packed_w, grad_out_w),
        (grad_up, grad_down),
        norm_grads,
    )


def adam_update(weight, first, second, gradient, rate):
    first = beta_one * first + (1.0 - beta_one) * gradient
    second = beta_two * second + (1.0 - beta_two) * gradient * gradient
    fix_one = 1.0 - beta_one**STEP
    fix_two = 1.0 - beta_two**STEP
    step_dir = first / fix_one / (jnp.sqrt(second / fix_two) + adam_eps)
    return (weight - rate * (step_dir + decay_rate * weight), first, second)


def own_rows(array):
    pieces = lax.axis_size(TENSOR)
    rows = array.shape[0] // pieces
    return lax.dynamic_slice_in_dim(array, lax.axis_index(TENSOR) * rows, rows, 0)


def swap(array, axis, step):
    size = lax.axis_size(axis)
    return lax.ppermute(array, axis, [(i, i ^ step) for i in range(size)])


def gather_axis(array, axis, place):
    array = jnp.expand_dims(array, place)
    step = 1
    while step < lax.axis_size(axis):
        other = swap(array, axis, step)
        upper = (lax.axis_index(axis) // step) % 2 == 1
        array = jnp.concatenate(
            [jnp.where(upper, other, array), jnp.where(upper, array, other)], axis=place
        )
        step *= 2
    return array


def gather_relative(arrays, axis):
    step = 1
    while step < lax.axis_size(axis):
        arrays = arrays + [swap(member, axis, step) for member in arrays]
        step *= 2
    return arrays


def reduce_axis(array, axis, place):
    size = lax.axis_size(axis)
    mine = lax.axis_index(axis)
    pick = partial(lax.dynamic_index_in_dim, axis=place, keepdims=False)
    if size <= 4:
        parts = [
            swap(pick(array, mine ^ step).astype(low), axis, step) for step in range(1, size)
        ]
        return sum([part.astype(jnp.float32) for part in parts], pick(array, mine))
    step = size // 2
    while step >= 1:
        shape = array.shape
        array = array.reshape(shape[:place] + (2, step) + shape[place + 1 :])
        upper = (mine // step) % 2
        other = swap(pick(array, 1 - upper).astype(low), axis, step)
        array = pick(array, upper) + other.astype(jnp.float32)
        step //= 2
    return lax.squeeze(array, (place,))


def reduce_relative(arrays, axis):
    step = lax.axis_size(axis) // 2
    while step >= 1:
        half = len(arrays) // 2
        others = [swap(member.astype(low), axis, step) for member in arrays[half:]]
        arrays = [
            member.astype(jnp.float32) + other.astype(jnp.float32)
            for member, other in zip(arrays[:half], others)
        ]
        step //= 2
    return arrays


def gather_mats(piece, pair_first):
    rows, columns = piece.shape
    whole = lax.all_gather(piece, "heads", axis=0, tiled=False)
    if pair_first:
        whole = gather_axis(gather_axis(whole, "pair", 1), "shard", 0)
    else:
        whole = gather_axis(gather_axis(whole, "shard", 0), "pair", 2)
    return gather_axis(whole, "core", 3).reshape(-1, columns)


def gather_feed(piece, pair_first):
    rows, columns = piece.shape
    whole = lax.all_gather(piece, "heads", axis=0, tiled=False)
    if pair_first:
        blocks = gather_relative([whole], "pair")
        blocks = [gather_axis(member, "shard", 0) for member in blocks]
    else:
        blocks = gather_relative([gather_axis(whole, "shard", 0)], "pair")
    blocks = gather_relative(blocks, "core")
    return [member.reshape(-1, columns) for member in blocks]


def scatter_mats(gradient, pair_first):
    shard, heads, pair, core = (lax.axis_size(axis) for axis in AXES)
    columns = gradient.shape[-1]
    gradient = gradient.reshape(shard, heads, pair, core, -1, columns)
    gradient = reduce_axis(gradient, "core", 3)
    if pair_first:
        gradient = reduce_axis(reduce_axis(gradient, "pair", 2), "shard", 0)
    else:
        gradient = reduce_axis(reduce_axis(gradient, "shard", 0), "pair", 1)
    return reduce_axis(gradient, "heads", 0)


def scatter_feed(blocks, pair_first):
    shard, heads = (lax.axis_size(axis) for axis in AXES[:2])
    columns = blocks[0].shape[-1]
    blocks = reduce_relative(blocks, "core")
    blocks = [member.reshape(shard, heads, -1, columns) for member in blocks]
    if pair_first:
        (gradient,) = reduce_relative(blocks, "pair")
        gradient = reduce_axis(gradient, "shard", 0)
    else:
        blocks = [reduce_axis(member, "shard", 0) for member in blocks]
        (gradient,) = reduce_relative(blocks, "pair")
    return reduce_axis(gradient, "heads", 0)


def gather_owned(piece):
    whole = gather_axis(gather_axis(piece, "pair", 0), "core", 1)
    return whole.reshape(-1, piece.shape[-1])


def butterfly_sum(values):
    for axis in ("core", "pair", "shard", "heads"):
        step = 1
        while step < lax.axis_size(axis):
            values = values + swap(values, axis, step)
            step *= 2
    return values


def per_device(
    patch_pixels,
    keep_index,
    restore_index,
    masked,
    encoder_mats,
    encoder_mats_first,
    encoder_mats_second,
    decoder_mats,
    decoder_mats_first,
    decoder_mats_second,
    encoder_feed,
    encoder_feed_first,
    encoder_feed_second,
    decoder_feed,
    decoder_feed_first,
    decoder_feed_second,
    encoder_norms,
    encoder_norms_first,
    encoder_norms_second,
    decoder_norms,
    decoder_norms_first,
    decoder_norms_second,
):
    masters = (encoder_mats, decoder_mats, encoder_feed, decoder_feed, encoder_norms, decoder_norms)
    firsts = (
        encoder_mats_first,
        decoder_mats_first,
        encoder_feed_first,
        decoder_feed_first,
        encoder_norms_first,
        decoder_norms_first,
    )
    seconds = (
        encoder_mats_second,
        decoder_mats_second,
        encoder_feed_second,
        decoder_feed_second,
        encoder_norms_second,
        decoder_norms_second,
    )
    rates = (learn_rate, learn_rate, learn_rate, learn_rate, norm_rate, norm_rate)
    groups = lax.axis_size("shard") * lax.axis_size("heads")
    pieces = lax.axis_size(TENSOR)
    devices = groups * pieces

    patch_pixels = own_rows(patch_pixels)
    keep_index = own_rows(keep_index)
    restore_index = own_rows(restore_index)
    masked = own_rows(masked)
    images, patches, pixel_dim = patch_pixels.shape
    kept = keep_index.shape[1]

    enc_rows, enc_cols = encoder_mats.shape
    dec_rows, dec_cols = decoder_mats.shape
    width_enc = enc_rows * groups
    width_dec = dec_rows * groups
    enc_part = enc_rows // pieces
    enc_norm_size = encoder_norms.size
    dec_norm_size = decoder_norms.size
    small = enc_norm_size + dec_norm_size
    extra = -(-small // (enc_part * 128)) * 128

    tables = jnp.concatenate([encoder_norms.reshape(-1), decoder_norms.reshape(-1)])
    tables = jnp.pad(tables, (0, enc_part * extra - small)).reshape(enc_part, extra)
    enc_send = own_rows(encoder_mats).astype(low)
    head_cols = 4 * width_enc
    tail_send = jnp.concatenate([enc_send[:, head_cols:], tables.astype(low)], axis=1)
    enc_head = gather_mats(enc_send[:, :head_cols], True)
    enc_tail = gather_mats(tail_send, False)
    feed = encoder_feed.astype(low)
    enc_feed = (gather_feed(feed[0], False), gather_feed(feed[1], True))
    dec_w = gather_mats(own_rows(decoder_mats).astype(low), False)
    feed = decoder_feed.astype(low)
    dec_feed = (gather_feed(feed[0], True), gather_feed(feed[1], False))

    tail_cols = enc_cols - head_cols
    tables = enc_tail[:, tail_cols:].reshape(groups, pieces, enc_part * extra)[:, 0, :small]
    enc_norm = tables[:, :enc_norm_size].reshape(groups, -1, enc_rows).transpose(1, 0, 2)
    enc_norm = enc_norm.reshape(-1, width_enc).astype(jnp.float32)
    dec_norm = tables[:, enc_norm_size:].reshape(groups, -1, dec_rows).transpose(1, 0, 2)
    dec_norm = dec_norm.reshape(-1, width_dec).astype(jnp.float32)

    emb_w = enc_head[:, :width_enc]
    enc_packed = enc_head[:, width_enc:]
    enc_out = enc_tail[:, :width_enc]
    proj_w = enc_tail[:, width_enc:tail_cols]
    dec_packed = dec_w[:, : 3 * width_dec]
    dec_out = dec_w[:, 3 * width_dec : 4 * width_dec]
    pixel_w = dec_w[:, 4 * width_dec :]

    picked = jnp.take_along_axis(patch_pixels, keep_index[:, :, None], axis=1).reshape(
        images * kept, pixel_dim
    )
    stream = (
        product(picked, emb_w).reshape(images, kept, width_enc)
        + jnp.asarray(positions(patches, width_enc))[keep_index]
    )
    stream, enc_saved = layer_forward(stream, enc_packed, enc_out, enc_feed, enc_norm, HEADS_E)
    enc_flat = stream.reshape(images * kept, width_enc)
    enc_final = layer_norm(enc_flat, enc_norm[4], enc_norm[5]).astype(low)
    latent = product(enc_final, proj_w).reshape(images, kept, width_dec)
    filler = jnp.broadcast_to(dec_norm[6], (images, patches - kept, width_dec))
    whole = jnp.concatenate([latent, filler], axis=1)
    stream = jnp.take_along_axis(whole, restore_index[:, :, None], axis=1) + jnp.asarray(
        positions(patches, width_dec)
    )
    stream, dec_saved = layer_forward(stream, dec_packed, dec_out, dec_feed, dec_norm, HEADS_D)
    dec_flat = stream.reshape(images * patches, width_dec)
    dec_final = layer_norm(dec_flat, dec_norm[4], dec_norm[5]).astype(low)
    prediction = product(dec_final, pixel_w)
    errors = prediction - patch_pixels.reshape(images * patches, pixel_dim).astype(jnp.float32)
    chosen_rows = masked.reshape(images * patches, 1).astype(jnp.float32)
    scaling = 1.0 / (images * devices * (patches - kept) * pixel_dim)
    loss_local = jnp.sum(chosen_rows * errors * errors) * scaling

    grad_pred = (2.0 * scaling * chosen_rows * errors).astype(low)
    grad_pixel_w = product_left(dec_final, grad_pred)
    grad_final = product_right(grad_pred, pixel_w)
    final_pull = jax.vjp(layer_norm, dec_flat, dec_norm[4], dec_norm[5])[1]
    grad_stream, dec_gain_three, dec_shift_three = final_pull(grad_final)
    grad_stream, dec_mats_grad, dec_feed_grad, dec_norm_grad = layer_backward(
        grad_stream, dec_saved, dec_packed, dec_out, dec_feed, dec_norm, HEADS_D
    )
    dec_feed_sum = jnp.stack(
        [scatter_feed(dec_feed_grad[0], True), scatter_feed(dec_feed_grad[1], False)]
    )
    grad_dec_mats = jnp.concatenate([dec_mats_grad[0], dec_mats_grad[1], grad_pixel_w], axis=1)
    dec_mats_sum = scatter_mats(grad_dec_mats, False)

    grad_cube = grad_stream.reshape(images, patches, width_dec)
    grad_latent = (
        jnp.take_along_axis(grad_cube, keep_index[:, :, None], axis=1)
        .reshape(images * kept, width_dec)
        .astype(low)
    )
    grad_mask = jnp.sum(grad_cube * masked[:, :, None].astype(jnp.float32), axis=(0, 1))
    grad_proj = product_left(enc_final, grad_latent)
    grad_final = product_right(grad_latent, proj_w)
    final_pull = jax.vjp(layer_norm, enc_flat, enc_norm[4], enc_norm[5])[1]
    grad_stream, enc_gain_three, enc_shift_three = final_pull(grad_final)
    grad_stream, enc_mats_grad, enc_feed_grad, enc_norm_grad = layer_backward(
        grad_stream, enc_saved, enc_packed, enc_out, enc_feed, enc_norm, HEADS_E
    )
    enc_feed_sum = jnp.stack(
        [scatter_feed(enc_feed_grad[0], False), scatter_feed(enc_feed_grad[1], True)]
    )
    grad_embed = product_left(picked, grad_stream.astype(low))
    grad_enc_norms = jnp.concatenate(
        [enc_norm_grad, jnp.stack([enc_gain_three, enc_shift_three])], axis=0
    )
    grad_dec_norms = jnp.concatenate(
        [dec_norm_grad, jnp.stack([dec_gain_three, dec_shift_three, grad_mask])], axis=0
    )
    tables = jnp.concatenate(
        [
            grad_enc_norms.reshape(-1, groups, enc_rows).transpose(1, 0, 2).reshape(groups, -1),
            grad_dec_norms.reshape(-1, groups, dec_rows).transpose(1, 0, 2).reshape(groups, -1),
        ],
        axis=1,
    )
    tables = jnp.pad(tables, ((0, 0), (0, enc_part * extra - small)))
    tables = jnp.pad(tables[:, None], ((0, 0), (0, pieces - 1), (0, 0)))
    tables = tables.reshape(width_enc, extra)
    enc_head_sum = scatter_mats(jnp.concatenate([grad_embed, enc_mats_grad[0]], axis=1), True)
    enc_tail_sum = scatter_mats(
        jnp.concatenate([enc_mats_grad[1], grad_proj, tables], axis=1), False
    )
    squares = sum(
        jnp.sum(jnp.square(member))
        for member in (enc_feed_sum, dec_feed_sum, dec_mats_sum, enc_head_sum, enc_tail_sum)
    )
    totals = butterfly_sum(jnp.stack([loss_local, squares]))
    enc_head_full = gather_owned(enc_head_sum)
    enc_tail_full = gather_owned(enc_tail_sum)
    tables = enc_tail_full[:enc_part, tail_cols:].reshape(-1)[:small]
    reduced = (
        jnp.concatenate([enc_head_full, enc_tail_full[:, :tail_cols]], axis=1),
        gather_owned(dec_mats_sum),
        enc_feed_sum,
        dec_feed_sum,
        tables[:enc_norm_size].reshape(encoder_norms.shape),
        tables[enc_norm_size:].reshape(decoder_norms.shape),
    )
    loss = totals[0]
    norm = jnp.sqrt(totals[1])
    factor = clip_limit / jnp.maximum(norm, clip_limit)
    results = [loss, norm]
    for weight, first, second, gradient, rate in zip(masters, firsts, seconds, reduced, rates):
        results.extend(adam_update(weight, first, second, gradient * factor, rate))
    return tuple(results)


def solution(mesh):
    shard, heads, tensor = (mesh.shape[axis] for axis in ("shard", "heads", "tensor"))
    mesh = Mesh(mesh.devices.reshape(shard, heads, tensor // 2, 2), AXES)
    rows = P(("shard", "heads"), None)
    feeds = P(None, ("shard", "heads"), TENSOR)
    norms = P(None, ("shard", "heads"))
    states = (rows,) * 6 + (feeds,) * 6 + (norms,) * 6
    return jax.shard_map(
        per_device,
        mesh=mesh,
        in_specs=(P(("shard", "heads"), None, None), rows, rows, rows) + states,
        out_specs=(P(), P()) + states,
        check_vma=False,
    )
```

```python
from functools import partial
import math

import jax
import jax.numpy as jnp
import numpy as np
from jax import lax
from jax.experimental import pallas as pl
from jax.experimental.pallas import tpu as pltpu
from jax.sharding import Mesh, PartitionSpec as P

HEADS_E = 12
HEADS_D = 16
STEP = 5

clip_limit = 0.01
beta_one = 0.9
beta_two = 0.999
learn_rate = 0.05
norm_rate = 0.5
decay_rate = 0.05
adam_eps = 1e-08
norm_eps = 1e-06

AXES = ("shard", "heads", "pair", "core")
TENSOR = ("pair", "core")
low = jnp.bfloat16


def positions(places, features):
    where = np.arange(places, dtype=np.float32)[:, None]
    column = np.arange(features // 2, dtype=np.float32)[None, :]
    angles = where * np.exp(column * np.float32(-2.0 * math.log(10000.0) / features))
    return np.concatenate([np.sin(angles), np.cos(angles)], axis=1).astype(np.float32)


def layer_norm(rows, gain, shift):
    centered = rows - jnp.mean(rows, axis=-1, keepdims=True)
    spread = jnp.mean(centered * centered, axis=-1, keepdims=True)
    return centered * lax.rsqrt(spread + norm_eps) * gain + shift


def product(left, right):
    return jnp.dot(left, right, preferred_element_type=jnp.float32)


def product_left(left, right):
    return lax.dot_general(
        left, right, (((0,), (0,)), ((), ())), preferred_element_type=jnp.float32
    )


def product_right(left, right):
    return lax.dot_general(
        left, right, (((1,), (1,)), ((), ())), preferred_element_type=jnp.float32
    )


def norm_forward(rows, gain, shift):
    centered = rows - jnp.mean(rows, axis=-1, keepdims=True)
    scale = lax.rsqrt(jnp.mean(centered * centered, axis=-1, keepdims=True) + norm_eps)
    return centered * scale * gain + shift


def norm_backward(rows, gain, gradient):
    centered = rows - jnp.mean(rows, axis=-1, keepdims=True)
    scale = lax.rsqrt(jnp.mean(centered * centered, axis=-1, keepdims=True) + norm_eps)
    unit = centered * scale
    inner = gradient * gain
    back = inner - jnp.mean(inner, axis=-1, keepdims=True)
    back = (back - unit * jnp.mean(inner * unit, axis=-1, keepdims=True)) * scale
    gains = jnp.sum(gradient * unit, axis=0, keepdims=True)
    return back, gains, jnp.sum(gradient, axis=0, keepdims=True)


def key_mask(rows, image_rows, valid):
    row = lax.broadcasted_iota(jnp.int32, (rows, rows), 0)
    column = lax.broadcasted_iota(jnp.int32, (rows, rows), 1)
    if rows == image_rows:
        return column < valid
    mask = None
    for start in range(0, rows, image_rows):
        inside = (row >= start) & (row < start + image_rows)
        inside = inside & (column >= start) & (column < start + valid)
        mask = inside if mask is None else mask | inside
    return mask


def head_lanes(rows, head_size):
    lane = lax.broadcasted_iota(jnp.int32, (rows, 128), 1)
    return [
        jnp.where((lane >= start) & (lane < start + head_size), 1.0, 0.0).astype(low)
        for start in range(0, 128, head_size)
    ]


def softmax_rows(queries, key_rows, mask, score_scale):
    scores = product_right(queries, key_rows) * score_scale
    scores = jnp.where(mask, scores, -1e30)
    powers = jnp.exp(scores - jnp.max(scores, axis=-1, keepdims=True))
    return powers * (1.0 / jnp.sum(powers, axis=-1, keepdims=True))


def chunk_of(size):
    return 512 if size % 512 == 0 else 256 if size % 256 == 0 else size


def layer_kernel(
    image_rows, valid, head_size, x, packed_w, out_w, up0, up1, down0, down1, norms,
    result, normed, packed, merged, mixed, second, pre0, pre1, hidden0, hidden1,
):
    rows, width = x.shape
    normed[...] = norm_forward(x[...], norms[0:1, :], norms[1:2, :]).astype(low)

    @pl.loop(0, 3)
    def _(part):
        columns = pl.ds(pl.multiple_of(part * width, 128), width)
        packed[:, columns] = product(normed[...], packed_w[:, columns]).astype(low)

    @pl.loop(0, width // 128)
    def _(group):
        mask = key_mask(rows, image_rows, valid)
        base = group * 128
        queries, key_rows, value_rows = (
            packed[:, pl.ds(pl.multiple_of(part * width + base, 128), 128)] for part in range(3)
        )
        total = jnp.zeros((rows, 128), jnp.float32)
        for lanes in head_lanes(rows, head_size):
            shares = softmax_rows(queries * lanes, key_rows, mask, head_size ** (-0.5))
            total = total + product(shares.astype(low), value_rows * lanes)
        merged[:, pl.ds(pl.multiple_of(base, 128), 128)] = total.astype(low)

    mixed[...] = x[...] + product(merged[...], out_w[...])
    second[...] = norm_forward(mixed[...], norms[2:3, :], norms[3:4, :]).astype(low)
    result[...] = mixed[...]
    for up, down, pre, hidden in ((up0, down0, pre0, hidden0), (up1, down1, pre1, hidden1)):
        size = chunk_of(up.shape[1])

        @pl.loop(0, up.shape[1] // size)
        def _(part):
            columns = pl.ds(pl.multiple_of(part * size, 128), size)
            value = product(second[...], up[:, columns])
            pre[:, columns] = value
            half = 0.5 * (1.0 + lax.erf(value * math.sqrt(0.5)))
            units = (value * half).astype(low)
            hidden[:, columns] = units
            result[...] += product_right(units, down[:, columns])


def feed_kernel(
    gradient, mixed, pre0, pre1, up0, up1, down0, down1, norms,
    grad_mixed, branch, attn, grad_pre0, grad_pre1, norm_grads, total,
):
    branch[...] = gradient[...].astype(low)
    total[...] = jnp.zeros_like(total)
    for up, down, pre, grad_pre in ((up0, down0, pre0, grad_pre0), (up1, down1, pre1, grad_pre1)):
        size = chunk_of(up.shape[1])

        @pl.loop(0, up.shape[1] // size)
        def _(part):
            columns = pl.ds(pl.multiple_of(part * size, 128), size)
            value = pre[:, columns]
            slope = 0.5 * (1.0 + lax.erf(value * math.sqrt(0.5)))
            slope += value * jnp.exp(-0.5 * value * value) * (1.0 / math.sqrt(2.0 * math.pi))
            units = (product(branch[...], down[:, columns]) * slope).astype(low)
            grad_pre[:, columns] = units
            total[...] += product_right(units, up[:, columns])

    back, gains, shifts = norm_backward(mixed[...], norms[2:3, :], total[...])
    back = back + gradient[...]
    grad_mixed[...] = back
    attn[...] = back.astype(low)
    norm_grads[0:1, :] = gains
    norm_grads[1:2, :] = shifts


def attention_kernel(
    image_rows, valid, head_size, grad_mixed, attn, x, packed, packed_w, out_w, norms,
    grad_x, grad_packed, norm_grads, grad_merged,
):
    rows, width = x.shape
    score_scale = head_size ** (-0.5)
    grad_merged[...] = product_right(attn[...], out_w[...]).astype(low)

    @pl.loop(0, width // 128)
    def _(group):
        mask = key_mask(rows, image_rows, valid)
        base = group * 128
        places = [pl.ds(pl.multiple_of(part * width + base, 128), 128) for part in range(3)]
        queries, key_rows, value_rows = (packed[:, place] for place in places)
        grad_out = grad_merged[:, pl.ds(pl.multiple_of(base, 128), 128)]
        totals = [jnp.zeros((rows, 128), jnp.float32)] * 3
        for lanes in head_lanes(rows, head_size):
            own_queries, own_out = queries * lanes, grad_out * lanes
            shares = softmax_rows(own_queries, key_rows, mask, score_scale)
            grad_shares = product_right(own_out, value_rows)
            inner = jnp.sum(shares * grad_shares, axis=-1, keepdims=True)
            grad_scores = (shares * (grad_shares - inner)).astype(low)
            totals = [
                totals[0] + product(grad_scores, key_rows * lanes),
                totals[1] + product_left(grad_scores, own_queries),
                totals[2] + product_left(shares.astype(low), own_out),
            ]
        scales = (score_scale, score_scale, 1.0)
        for place, total, scale in zip(places, totals, scales):
            grad_packed[:, place] = (total * scale).astype(low)

    grad_normed = product_right(grad_packed[...], packed_w[...])
    back, gains, shifts = norm_backward(x[...], norms[0:1, :], grad_normed)
    grad_x[...] = back + grad_mixed[...]
    norm_grads[0:1, :] = gains
    norm_grads[1:2, :] = shifts


def loss_kernel(
    scaling, x, pixels, chosen, pixel_w, norms, final, grad_pred, grad_x, norm_grads, loss
):
    final[...] = norm_forward(x[...], norms[4:5, :], norms[5:6, :]).astype(low)
    errors = product(final[...], pixel_w[...]) - pixels[...].astype(jnp.float32)
    errors = errors * chosen[...]
    loss[...] = jnp.broadcast_to(jnp.sum(errors * errors) * scaling, loss.shape)
    grad_pred[...] = (errors * (2.0 * scaling)).astype(low)
    grad_final = product_right(grad_pred[...], pixel_w[...])
    back, gains, shifts = norm_backward(x[...], norms[4:5, :], grad_final)
    grad_x[...] = back
    norm_grads[0:1, :] = gains
    norm_grads[1:2, :] = shifts


def call_blocks(kernel, block, blocked, whole, outs, scratch=(), flops=0):
    steps = blocked[0].shape[0] // block
    specs = [pl.BlockSpec((block, member.shape[1]), lambda i: (i, 0)) for member in blocked]
    specs += [
        pl.BlockSpec(member.shape, lambda i: (0, 0), pipeline_mode=pl.Buffered(1))
        for member in whole
    ]
    shapes = [jax.ShapeDtypeStruct((rows * steps, columns), kind) for rows, columns, kind in outs]
    size = sum(member.size * member.dtype.itemsize for member in (*blocked, *whole, *shapes))
    return pl.pallas_call(
        kernel,
        grid=(steps,),
        in_specs=specs,
        out_specs=[pl.BlockSpec((rows, columns), lambda i: (i, 0)) for rows, columns, _ in outs],
        out_shape=shapes,
        scratch_shapes=list(scratch),
        compiler_params=pltpu.CompilerParams(vmem_limit_bytes=60 << 20),
        cost_estimate=pl.CostEstimate(flops=flops, bytes_accessed=size, transcendentals=0),
    )(*blocked, *whole)


def layer_forward(stream, packed_w, out_w, feed, norms, head_count, block, image_rows, valid):
    rows, width = stream.shape
    units = feed[0][0].shape[1]
    outs = [
        (block, width, jnp.float32),
        (block, width, low),
        (block, 3 * width, low),
        (block, width, low),
        (block, width, jnp.float32),
        (block, width, low),
        (block, units, jnp.float32),
        (block, units, jnp.float32),
        (block, units, low),
        (block, units, low),
    ]
    return call_blocks(
        partial(layer_kernel, image_rows, valid, width // head_count),
        block,
        [stream],
        [packed_w, out_w, *feed[0], *feed[1], norms],
        outs,
        flops=2 * rows * width * (4 * width + 4 * units + 2 * block),
    )


def feed_backward(gradient, saved, feed, norms, block):
    _, normed, packed, merged, mixed, second, pre0, pre1, hidden0, hidden1 = saved
    rows, width = gradient.shape
    units = pre0.shape[1]
    grad_mixed, branch, attn, grad_pre0, grad_pre1, norm_grads = call_blocks(
        feed_kernel,
        block,
        [gradient, mixed, pre0, pre1],
        [*feed[0], *feed[1], norms],
        [
            (block, width, jnp.float32),
            (block, width, low),
            (block, width, low),
            (block, units, low),
            (block, units, low),
            (8, width, jnp.float32),
        ],
        [pltpu.VMEM((block, width), jnp.float32)],
        flops=8 * rows * width * units,
    )
    grad_down = (product_left(branch, hidden0), product_left(branch, hidden1).astype(low))
    grad_up = (product_left(second, grad_pre0), product_left(second, grad_pre1).astype(low))
    return grad_mixed, attn, grad_down, grad_up, norm_rows(norm_grads)


def attention_backward(
    grad_mixed, attn, stream, saved, packed_w, out_w, norms, head_count, block, image_rows, valid
):
    _, normed, packed, merged, mixed, second, pre0, pre1, hidden0, hidden1 = saved
    rows, width = stream.shape
    grad_x, grad_packed, norm_grads = call_blocks(
        partial(attention_kernel, image_rows, valid, width // head_count),
        block,
        [grad_mixed, attn, stream, packed],
        [packed_w, out_w, norms],
        [(block, width, jnp.float32), (block, 3 * width, low), (8, width, jnp.float32)],
        [pltpu.VMEM((block, width), low)],
        flops=2 * rows * width * (4 * width + 5 * block),
    )
    return grad_x, split_grad(normed, grad_packed), split_grad(merged, attn), norm_rows(norm_grads)


def norm_rows(partial_sums):
    sums = jnp.sum(partial_sums.reshape(-1, 8, partial_sums.shape[1]), axis=0)
    return sums[0], sums[1]


def adam_update(weight, first, second, gradient, rate):
    first = beta_one * first + (1.0 - beta_one) * gradient
    second = beta_two * second + (1.0 - beta_two) * gradient * gradient
    fix_one = 1.0 - beta_one**STEP
    fix_two = 1.0 - beta_two**STEP
    step_dir = first / fix_one / (jnp.sqrt(second / fix_two) + adam_eps)
    return (weight - rate * (step_dir + decay_rate * weight), first, second)


def own_rows(array):
    pieces = lax.axis_size(TENSOR)
    rows = array.shape[0] // pieces
    return lax.dynamic_slice_in_dim(array, lax.axis_index(TENSOR) * rows, rows, 0)


def after(value, *others):
    if not others:
        return value
    zero = sum(other[(0,) * other.ndim].astype(jnp.float32) for other in others) * 0.0
    return value + zero.astype(value.dtype)


class Links:
    def swap(self, array, axis, step):
        return swap(array, axis, step)


class Job:
    def __init__(self, steps):
        self.steps, self.result, self.ended = steps, None, False
        self.received = []

    def go(self, count=1):
        for _ in range(count):
            if self.ended:
                return
            try:
                self.received.append(next(self.steps))
            except StopIteration as stop:
                self.result, self.ended = stop.value, True

    def finish(self):
        while not self.ended:
            self.go()
        return self.result


def swap(array, axis, step):
    size = lax.axis_size(axis)
    return lax.ppermute(array, axis, [(i, i ^ step) for i in range(size)])


def halves(array):
    second = lax.axis_index("core") == 1
    half = array.shape[-1] // 2
    lower, upper = array[:, :half], array[:, half:]
    return jnp.where(second, upper, lower), jnp.where(second, lower, upper)


def join_halves(own, other):
    second = lax.axis_index("core") == 1
    return jnp.concatenate(
        [jnp.where(second, other, own), jnp.where(second, own, other)], axis=-1
    )


def gather_axis(links, array, axis, place):
    size = lax.axis_size(axis)
    step, at = size // 2, place
    while step >= 1:
        array = jnp.expand_dims(array, at)
        other = links.swap(array, axis, step)
        yield other
        upper = (lax.axis_index(axis) // step) % 2 == 1
        array = jnp.concatenate(
            [jnp.where(upper, other, array), jnp.where(upper, array, other)], axis=at
        )
        at += 1
        step //= 2
    return array.reshape(array.shape[:place] + (size,) + array.shape[at:])


def gather_rows(links, piece, shard_first=False):
    columns = piece.shape[1:]
    if shard_first:
        whole = yield from gather_axis(links, piece, "shard", 0)
        whole = yield from gather_axis(links, whole, "heads", 1)
    else:
        whole = yield from gather_axis(links, piece, "heads", 0)
        whole = yield from gather_axis(links, whole, "shard", 0)
    return whole.reshape((-1,) + columns)


def gather_mats(links, matrices):
    send = jnp.concatenate([halves(member)[0] for member in matrices], axis=1).astype(low)
    own = yield from gather_rows(links, send)
    other = links.swap(own, "core", 1)
    yield other
    results, at = [], 0
    for member in matrices:
        until = at + member.shape[1] // 2
        results.append(join_halves(own[:, at:until], other[:, at:until]))
        at = until
    return results


def gather_feed(links, piece, shard_first):
    whole = yield from gather_rows(links, piece, shard_first)
    step = 1
    while step < lax.axis_size("pair"):
        other = links.swap(whole, "pair", step)
        yield other
        whole = jnp.concatenate([whole, other], axis=1)
        step *= 2
    other = links.swap(whole, "core", 1)
    yield other
    return [whole, other]


def reduce_axis(links, arrays, axis, place):
    size = lax.axis_size(axis)
    bits = size.bit_length() - 1
    mine = lax.axis_index(axis)
    arrays = [
        member.reshape(member.shape[:place] + (2,) * bits + member.shape[place + 1 :])
        for member in arrays
    ]
    for bit in range(bits):
        pick = partial(lax.dynamic_index_in_dim, axis=place + bits - 1 - bit, keepdims=False)
        upper = (mine >> bit) % 2
        send = [pick(member, 1 - upper).astype(low) for member in arrays]
        send = jnp.concatenate(send, axis=-1) if len(send) > 1 else send[0]
        keep = [pick(member, upper) for member in arrays]
        keep = jnp.concatenate(keep, axis=-1) if len(keep) > 1 else keep[0]
        other = links.swap(send, axis, 1 << bit)
        yield other
        arrays = [keep + other.astype(jnp.float32)]
    return arrays[0]


def split_grad(left, right):
    own, other = halves(right)
    return product_left(left, own), product_left(left, other).astype(low)


def scatter_mats(links, pairs):
    shard, heads = (lax.axis_size(axis) for axis in AXES[:2])
    others = [links.swap(send, "core", 1) for _, send in pairs]
    yield sum(other[:8, :128] for other in others)
    sums = [
        (own + other.astype(jnp.float32)).reshape(shard, heads, -1, own.shape[1])
        for (own, _), other in zip(pairs, others)
    ]
    total = yield from reduce_axis(links, sums, "shard", 0)
    total = yield from reduce_axis(links, [total], "heads", 0)
    step = 1
    while step < lax.axis_size("pair"):
        total = total.astype(low)
        other = links.swap(total, "pair", step)
        yield other
        total = total.astype(jnp.float32) + other.astype(jnp.float32)
        step *= 2
    return total


def scatter_feed(links, own, send):
    shard, heads, pair = (lax.axis_size(axis) for axis in AXES[:3])
    other = links.swap(send, "core", 1)
    yield other
    total = own + other.astype(jnp.float32)
    step = pair // 2
    while step >= 1:
        half = total.shape[1] // 2
        other = links.swap(total[:, half:].astype(low), "pair", step)
        yield other
        total = total[:, :half] + other.astype(jnp.float32)
        step //= 2
    total = total.reshape(shard, heads, -1, total.shape[1])
    total = yield from reduce_axis(links, [total], "shard", 0)
    return (yield from reduce_axis(links, [total], "heads", 0))


def butterfly_sum(values):
    for axis in AXES[::-1]:
        step = 1
        while step < lax.axis_size(axis):
            values = values + swap(values, axis, step)
            step *= 2
    return values


def per_device(
    patch_pixels,
    keep_index,
    restore_index,
    masked,
    encoder_mats,
    encoder_mats_first,
    encoder_mats_second,
    decoder_mats,
    decoder_mats_first,
    decoder_mats_second,
    encoder_feed,
    encoder_feed_first,
    encoder_feed_second,
    decoder_feed,
    decoder_feed_first,
    decoder_feed_second,
    encoder_norms,
    encoder_norms_first,
    encoder_norms_second,
    decoder_norms,
    decoder_norms_first,
    decoder_norms_second,
):
    masters = (encoder_mats, decoder_mats, encoder_feed, decoder_feed, encoder_norms, decoder_norms)
    firsts = (
        encoder_mats_first,
        decoder_mats_first,
        encoder_feed_first,
        decoder_feed_first,
        encoder_norms_first,
        decoder_norms_first,
    )
    seconds = (
        encoder_mats_second,
        decoder_mats_second,
        encoder_feed_second,
        decoder_feed_second,
        encoder_norms_second,
        decoder_norms_second,
    )
    rates = (learn_rate, learn_rate, learn_rate, learn_rate, norm_rate, norm_rate)
    groups = lax.axis_size("shard") * lax.axis_size("heads")
    pieces = lax.axis_size(TENSOR)
    devices = groups * pieces

    patch_pixels = own_rows(patch_pixels)
    keep_index = own_rows(keep_index)
    restore_index = own_rows(restore_index)
    masked = own_rows(masked)
    images, patches, pixel_dim = patch_pixels.shape
    kept = keep_index.shape[1]

    enc_rows, enc_cols = encoder_mats.shape
    dec_rows, dec_cols = decoder_mats.shape
    width_enc = enc_rows * groups
    width_dec = dec_rows * groups
    enc_size, dec_size = encoder_norms.size, decoder_norms.size
    tables = jnp.concatenate([encoder_norms.reshape(-1), decoder_norms.reshape(-1)])
    tables = jnp.pad(tables, (0, -tables.size % 1024)).reshape(1, -1, 128).astype(low)
    links = Links()
    tables = Job(gather_rows(Links(), tables)).finish().reshape(groups, -1)
    enc_norm = tables[:, :enc_size].reshape(groups, -1, enc_rows).transpose(1, 0, 2)
    enc_norm = enc_norm.reshape(-1, width_enc).astype(jnp.float32)
    dec_norm = tables[:, enc_size : enc_size + dec_size].reshape(groups, -1, dec_rows)
    dec_norm = dec_norm.transpose(1, 0, 2).reshape(-1, width_dec).astype(jnp.float32)

    enc_cuts = (0, width_enc, 4 * width_enc, 5 * width_enc, enc_cols)
    dec_cuts = (0, 3 * width_dec, 4 * width_dec, dec_cols)
    enc_parts = [encoder_mats[:, a:b] for a, b in zip(enc_cuts, enc_cuts[1:])]
    dec_parts = [decoder_mats[:, a:b] for a, b in zip(dec_cuts, dec_cuts[1:])]
    enc_up, enc_down = encoder_feed.astype(low)
    dec_up, dec_down = decoder_feed.astype(low)
    eh = Job(gather_mats(links, enc_parts[:2]))
    et = Job(gather_mats(links, enc_parts[2:]))
    eu = Job(gather_feed(links, enc_up, False))
    ed = Job(gather_feed(links, enc_down, True))
    dm = Job(gather_mats(links, dec_parts))
    du = Job(gather_feed(links, dec_up, False))
    dd = Job(gather_feed(links, dec_down, True))
    for job in (eh, ed, et, dd, eh, ed, et, eu, eh, ed, eu, et, dd, eu, ed, dm, dd, eu):
        job.go()
    for job in (dm, du, dd, dm, du, du, du):
        job.go()
    emb_w, enc_packed = eh.finish()
    enc_out, proj_w = et.finish()
    enc_feed = [eu.finish(), ed.finish()]
    dec_packed, dec_out, pixel_w = dm.finish()
    dec_feed = [du.finish(), dd.finish()]

    enc_pad = -(-kept // 64) * 64
    dec_pad = -(-patches // 16) * 16
    keep_pad = jnp.pad(keep_index, ((0, 0), (0, enc_pad - kept)), constant_values=-1)
    spots = jnp.arange(patches, dtype=jnp.int32)
    picks = (keep_pad[:, :, None] == spots).astype(low)
    picked = jnp.einsum("bkp,bpd->bkd", picks, patch_pixels, preferred_element_type=jnp.float32)
    picked = picked.astype(low).reshape(images * enc_pad, pixel_dim)
    places = jnp.asarray(positions(patches, width_enc))[jnp.maximum(keep_pad, 0)]
    enc_stream = product(picked, emb_w) + places.reshape(images * enc_pad, width_enc)
    enc_block = images * enc_pad
    enc_shape = (enc_block, enc_pad, kept)
    enc_saved = layer_forward(
        enc_stream, enc_packed, enc_out, enc_feed, enc_norm, HEADS_E, *enc_shape
    )
    enc_flat = enc_saved[0]
    enc_final = layer_norm(enc_flat, enc_norm[4], enc_norm[5]).astype(low)
    latent = product(enc_final, proj_w).reshape(images, enc_pad, width_dec)
    restore_pad = jnp.pad(
        restore_index, ((0, 0), (0, dec_pad - patches)), constant_values=enc_pad + patches
    )
    slots = jnp.arange(enc_pad, dtype=jnp.int32)
    seen = restore_pad[:, :, None] < kept
    routes = ((restore_pad[:, :, None] == slots) & seen).astype(jnp.float32)
    table = jnp.pad(positions(patches, width_dec), ((0, dec_pad - patches), (0, 0)))
    dec_stream = jnp.einsum("bpk,bkd->bpd", routes, latent, precision=lax.Precision.HIGHEST)
    dec_stream = dec_stream + jnp.where(seen, 0.0, dec_norm[6]) + table
    dec_stream = dec_stream.reshape(images * dec_pad, width_dec)
    dec_shape = (dec_pad, dec_pad, patches)
    dec_saved = layer_forward(
        dec_stream, dec_packed, dec_out, dec_feed, dec_norm, HEADS_D, *dec_shape
    )
    row_pad = ((0, 0), (0, dec_pad - patches))
    pixels = jnp.pad(patch_pixels, (*row_pad, (0, 0))).reshape(images * dec_pad, pixel_dim)
    chosen = jnp.pad(masked.astype(jnp.float32), row_pad)
    scaling = 1.0 / (images * devices * (patches - kept) * pixel_dim)
    dec_final, grad_pred, grad_stream, dec_third, losses = call_blocks(
        partial(loss_kernel, scaling),
        dec_pad,
        [dec_saved[0], pixels, chosen.reshape(images * dec_pad, 1)],
        [pixel_w, dec_norm],
        [
            (dec_pad, width_dec, low),
            (dec_pad, pixel_dim, low),
            (dec_pad, width_dec, jnp.float32),
            (8, width_dec, jnp.float32),
            (8, 128, jnp.float32),
        ],
        flops=4 * images * dec_pad * width_dec * pixel_dim,
    )
    dec_third = norm_rows(dec_third)
    loss_local = jnp.sum(losses.reshape(images, 8, 128)[:, 0, 0])
    grad_pixel_w = split_grad(dec_final, grad_pred)
    grad_mixed, attn, grad_down, grad_up, dec_second = feed_backward(
        grad_stream, dec_saved, dec_feed, dec_norm, dec_pad
    )
    dd = Job(scatter_feed(links, *grad_down))
    du = Job(scatter_feed(links, *grad_up))
    for job in (dd, du, dd, du):
        job.go()
    grad_stream, grad_packed_w, grad_out_w, dec_first = attention_backward(
        grad_mixed, attn, dec_stream, dec_saved, dec_packed, dec_out, dec_norm, HEADS_D, *dec_shape
    )
    dm = Job(scatter_mats(links, [grad_packed_w, grad_out_w, grad_pixel_w]))
    for job in (dd, dm, du, dm):
        job.go()

    grad_cube = grad_stream.reshape(images, dec_pad, width_dec)
    grad_latent = jnp.einsum(
        "bpk,bpd->bkd", routes, grad_cube, precision=lax.Precision.HIGHEST
    ).reshape(images * enc_pad, width_dec)
    grad_latent = grad_latent.astype(low)
    grad_mask = jnp.sum(jnp.where(seen, 0.0, grad_cube), axis=(0, 1))
    grad_proj = split_grad(enc_final, grad_latent)
    grad_final = product_right(grad_latent, proj_w)
    final_pull = jax.vjp(layer_norm, enc_flat, enc_norm[4], enc_norm[5])[1]
    grad_stream, *enc_third = final_pull(grad_final)
    grad_mixed, attn, grad_down, grad_up, enc_second = feed_backward(
        grad_stream, enc_saved, enc_feed, enc_norm, enc_block
    )
    ed = Job(scatter_feed(links, *grad_down))
    eu = Job(scatter_feed(links, *grad_up))
    for job in (ed, eu, ed, dd, dd, du, du, eu):
        job.go()
    for job in (dm, dm, dm):
        job.go()
    grad_stream, grad_packed_w, grad_out_w, enc_first = attention_backward(
        grad_mixed, attn, enc_stream, enc_saved, enc_packed, enc_out, enc_norm, HEADS_E, *enc_shape
    )
    grad_embed = split_grad(picked, grad_stream.astype(low))
    et = Job(scatter_mats(links, [grad_out_w, grad_proj]))
    eh = Job(scatter_mats(links, [grad_embed, grad_packed_w]))
    for job in (et, et, ed, et, et, eh, ed, eh, et, ed, eu, eh, eh, eu, eu, eh):
        job.go()
    dec_feed_sum = (du.finish(), dd.finish())
    dec_mats_sum = dm.finish()
    enc_tail_sum = et.finish()
    enc_feed_sum = (eu.finish(), ed.finish())
    enc_head_sum = eh.finish()

    norm_grads = [
        jnp.stack([*enc_first, *enc_second, *enc_third]),
        jnp.stack([*dec_first, *dec_second, *dec_third, grad_mask]),
    ]
    copies = lax.axis_size("pair")
    squares = sum(jnp.sum(jnp.square(member)) for member in (*enc_feed_sum, *dec_feed_sum))
    squares += sum(
        jnp.sum(jnp.square(member)) for member in (enc_tail_sum, enc_head_sum, dec_mats_sum)
    ) * (1.0 / copies)
    packed = jnp.concatenate(
        [member.reshape(-1) for member in norm_grads] + [jnp.stack([loss_local, squares])]
    )
    packed = jnp.pad(packed, (0, -packed.size % 1024)).reshape(-1, 128)
    packed = butterfly_sum(packed).reshape(-1)
    enc_total, dec_total = (member.size for member in norm_grads)
    both_total = enc_total + dec_total
    loss = packed[both_total]
    total = packed[both_total + 1] + jnp.sum(jnp.square(packed[:both_total]))
    group = lax.axis_index(("shard", "heads"))
    enc_norm_sum = packed[:enc_total].reshape(-1, groups, enc_rows)
    dec_norm_sum = packed[enc_total : enc_total + dec_total].reshape(-1, groups, dec_rows)
    enc_norm_sum = lax.dynamic_index_in_dim(enc_norm_sum, group, 1, keepdims=False)
    dec_norm_sum = lax.dynamic_index_in_dim(dec_norm_sum, group, 1, keepdims=False)

    def whole_columns(own, parts):
        own = after(own, enc_head_sum, enc_tail_sum)
        other = swap(own, "core", 1)
        results, at = [], 0
        for member in parts:
            until = at + member.shape[1] // 2
            results.append(join_halves(own[:, at:until], other[:, at:until]))
            at = until
        return results

    reduced = (
        jnp.concatenate(
            whole_columns(enc_head_sum, enc_parts[:2]) + whole_columns(enc_tail_sum, enc_parts[2:]),
            axis=1,
        ),
        jnp.concatenate(whole_columns(dec_mats_sum, dec_parts), axis=1),
        jnp.stack(enc_feed_sum),
        jnp.stack(dec_feed_sum),
        enc_norm_sum,
        dec_norm_sum,
    )
    norm = jnp.sqrt(total)
    factor = clip_limit / jnp.maximum(norm, clip_limit)
    results = [loss, norm]
    for weight, first, second, gradient, rate in zip(masters, firsts, seconds, reduced, rates):
        results.extend(adam_update(weight, first, second, gradient * factor, rate))
    return tuple(results)


def solution(mesh):
    shard, heads, tensor = (mesh.shape[axis] for axis in ("shard", "heads", "tensor"))
    mesh = Mesh(mesh.devices.reshape(shard, heads, tensor // 2, 2), AXES)
    rows = P(("shard", "heads"), None)
    feeds = P(None, ("shard", "heads"), TENSOR)
    norms = P(None, ("shard", "heads"))
    states = (rows,) * 6 + (feeds,) * 6 + (norms,) * 6
    return jax.shard_map(
        per_device,
        mesh=mesh,
        in_specs=(P(("shard", "heads"), None, None), rows, rows, rows) + states,
        out_specs=(P(), P()) + states,
        check_vma=False,
    )
```

```python
from functools import partial
import math

import jax
import jax.numpy as jnp
import numpy as np
from jax import lax
from jax.experimental import pallas as pl
from jax.experimental.pallas import tpu as pltpu
from jax.sharding import Mesh, PartitionSpec as P

HEADS_E = 12
HEADS_D = 16
STEP = 5

clip_limit = 0.01
beta_one = 0.9
beta_two = 0.999
learn_rate = 0.05
norm_rate = 0.5
decay_rate = 0.05
adam_eps = 1e-08
norm_eps = 1e-06

AXES = ("shard", "heads", "pair", "core")
TENSOR = ("pair", "core")
low = jnp.bfloat16


def positions(places, features):
    where = np.arange(places, dtype=np.float32)[:, None]
    column = np.arange(features // 2, dtype=np.float32)[None, :]
    angles = where * np.exp(column * np.float32(-2.0 * math.log(10000.0) / features))
    return np.concatenate([np.sin(angles), np.cos(angles)], axis=1).astype(np.float32)


def layer_norm(rows, gain, shift):
    centered = rows - jnp.mean(rows, axis=-1, keepdims=True)
    spread = jnp.mean(centered * centered, axis=-1, keepdims=True)
    return centered * lax.rsqrt(spread + norm_eps) * gain + shift


def product(left, right):
    return jnp.dot(left, right, preferred_element_type=jnp.float32)


def product_left(left, right):
    return lax.dot_general(
        left, right, (((0,), (0,)), ((), ())), preferred_element_type=jnp.float32
    )


def product_right(left, right):
    return lax.dot_general(
        left, right, (((1,), (1,)), ((), ())), preferred_element_type=jnp.float32
    )


def norm_forward(rows, gain, shift):
    centered = rows - jnp.mean(rows, axis=-1, keepdims=True)
    scale = lax.rsqrt(jnp.mean(centered * centered, axis=-1, keepdims=True) + norm_eps)
    return centered * scale * gain + shift


def norm_backward(rows, gain, gradient):
    centered = rows - jnp.mean(rows, axis=-1, keepdims=True)
    scale = lax.rsqrt(jnp.mean(centered * centered, axis=-1, keepdims=True) + norm_eps)
    unit = centered * scale
    inner = gradient * gain
    back = inner - jnp.mean(inner, axis=-1, keepdims=True)
    back = (back - unit * jnp.mean(inner * unit, axis=-1, keepdims=True)) * scale
    gains = jnp.sum(gradient * unit, axis=0, keepdims=True)
    return back, gains, jnp.sum(gradient, axis=0, keepdims=True)


def key_mask(rows, image_rows, valid):
    row = lax.broadcasted_iota(jnp.int32, (rows, rows), 0)
    column = lax.broadcasted_iota(jnp.int32, (rows, rows), 1)
    if rows == image_rows:
        return column < valid
    mask = None
    for start in range(0, rows, image_rows):
        inside = (row >= start) & (row < start + image_rows)
        inside = inside & (column >= start) & (column < start + valid)
        mask = inside if mask is None else mask | inside
    return mask


def head_lanes(rows, head_size):
    lane = lax.broadcasted_iota(jnp.int32, (rows, 128), 1)
    return [
        jnp.where((lane >= start) & (lane < start + head_size), 1.0, 0.0).astype(low)
        for start in range(0, 128, head_size)
    ]


def softmax_rows(queries, key_rows, mask, score_scale):
    scores = product_right(queries, key_rows) * score_scale
    scores = jnp.where(mask, scores, -1e30)
    powers = jnp.exp(scores - jnp.max(scores, axis=-1, keepdims=True))
    return powers * (1.0 / jnp.sum(powers, axis=-1, keepdims=True))


def chunk_of(size):
    return 512 if size % 512 == 0 else 256 if size % 256 == 0 else size


def layer_kernel(
    image_rows, valid, head_size, x, packed_w, out_w, up0, up1, down0, down1, norms,
    result, normed, packed, merged, mixed, second, pre0, pre1, hidden0, hidden1,
):
    rows, width = x.shape
    normed[...] = norm_forward(x[...], norms[0:1, :], norms[1:2, :]).astype(low)

    @pl.loop(0, 3)
    def _(part):
        columns = pl.ds(pl.multiple_of(part * width, 128), width)
        packed[:, columns] = product(normed[...], packed_w[:, columns]).astype(low)

    @pl.loop(0, width // 128)
    def _(group):
        mask = key_mask(rows, image_rows, valid)
        base = group * 128
        queries, key_rows, value_rows = (
            packed[:, pl.ds(pl.multiple_of(part * width + base, 128), 128)] for part in range(3)
        )
        total = jnp.zeros((rows, 128), jnp.float32)
        for lanes in head_lanes(rows, head_size):
            shares = softmax_rows(queries * lanes, key_rows, mask, head_size ** (-0.5))
            total = total + product(shares.astype(low), value_rows * lanes)
        merged[:, pl.ds(pl.multiple_of(base, 128), 128)] = total.astype(low)

    mixed[...] = x[...] + product(merged[...], out_w[...])
    second[...] = norm_forward(mixed[...], norms[2:3, :], norms[3:4, :]).astype(low)
    result[...] = mixed[...]
    for up, down, pre, hidden in ((up0, down0, pre0, hidden0), (up1, down1, pre1, hidden1)):
        size = chunk_of(up.shape[1])

        @pl.loop(0, up.shape[1] // size)
        def _(part):
            columns = pl.ds(pl.multiple_of(part * size, 128), size)
            value = product(second[...], up[:, columns])
            pre[:, columns] = value
            half = 0.5 * (1.0 + lax.erf(value * math.sqrt(0.5)))
            units = (value * half).astype(low)
            hidden[:, columns] = units
            result[...] += product_right(units, down[:, columns])


def feed_kernel(
    gradient, mixed, pre0, pre1, up0, up1, down0, down1, norms,
    grad_mixed, branch, attn, grad_pre0, grad_pre1, norm_grads, total,
):
    branch[...] = gradient[...].astype(low)
    total[...] = jnp.zeros_like(total)
    for up, down, pre, grad_pre in ((up0, down0, pre0, grad_pre0), (up1, down1, pre1, grad_pre1)):
        size = chunk_of(up.shape[1])

        @pl.loop(0, up.shape[1] // size)
        def _(part):
            columns = pl.ds(pl.multiple_of(part * size, 128), size)
            value = pre[:, columns]
            slope = 0.5 * (1.0 + lax.erf(value * math.sqrt(0.5)))
            slope += value * jnp.exp(-0.5 * value * value) * (1.0 / math.sqrt(2.0 * math.pi))
            units = (product(branch[...], down[:, columns]) * slope).astype(low)
            grad_pre[:, columns] = units
            total[...] += product_right(units, up[:, columns])

    back, gains, shifts = norm_backward(mixed[...], norms[2:3, :], total[...])
    back = back + gradient[...]
    grad_mixed[...] = back
    attn[...] = back.astype(low)
    norm_grads[0:1, :] = gains
    norm_grads[1:2, :] = shifts


def attention_kernel(
    image_rows, valid, head_size, grad_mixed, attn, x, packed, packed_w, out_w, norms,
    grad_x, grad_packed, norm_grads, grad_merged,
):
    rows, width = x.shape
    score_scale = head_size ** (-0.5)
    grad_merged[...] = product_right(attn[...], out_w[...]).astype(low)

    @pl.loop(0, width // 128)
    def _(group):
        mask = key_mask(rows, image_rows, valid)
        base = group * 128
        places = [pl.ds(pl.multiple_of(part * width + base, 128), 128) for part in range(3)]
        queries, key_rows, value_rows = (packed[:, place] for place in places)
        grad_out = grad_merged[:, pl.ds(pl.multiple_of(base, 128), 128)]
        totals = [jnp.zeros((rows, 128), jnp.float32)] * 3
        for lanes in head_lanes(rows, head_size):
            own_queries, own_out = queries * lanes, grad_out * lanes
            shares = softmax_rows(own_queries, key_rows, mask, score_scale)
            grad_shares = product_right(own_out, value_rows)
            inner = jnp.sum(shares * grad_shares, axis=-1, keepdims=True)
            grad_scores = (shares * (grad_shares - inner)).astype(low)
            totals = [
                totals[0] + product(grad_scores, key_rows * lanes),
                totals[1] + product_left(grad_scores, own_queries),
                totals[2] + product_left(shares.astype(low), own_out),
            ]
        scales = (score_scale, score_scale, 1.0)
        for place, total, scale in zip(places, totals, scales):
            grad_packed[:, place] = (total * scale).astype(low)

    grad_normed = product_right(grad_packed[...], packed_w[...])
    back, gains, shifts = norm_backward(x[...], norms[0:1, :], grad_normed)
    grad_x[...] = back + grad_mixed[...]
    norm_grads[0:1, :] = gains
    norm_grads[1:2, :] = shifts


def loss_kernel(
    scaling, x, pixels, chosen, pixel_w, norms, final, grad_pred, grad_x, norm_grads, loss
):
    final[...] = norm_forward(x[...], norms[4:5, :], norms[5:6, :]).astype(low)
    errors = product(final[...], pixel_w[...]) - pixels[...].astype(jnp.float32)
    errors = errors * chosen[...]
    loss[...] = jnp.broadcast_to(jnp.sum(errors * errors) * scaling, loss.shape)
    grad_pred[...] = (errors * (2.0 * scaling)).astype(low)
    grad_final = product_right(grad_pred[...], pixel_w[...])
    back, gains, shifts = norm_backward(x[...], norms[4:5, :], grad_final)
    grad_x[...] = back
    norm_grads[0:1, :] = gains
    norm_grads[1:2, :] = shifts


def call_blocks(kernel, block, blocked, whole, outs, scratch=(), flops=0):
    steps = blocked[0].shape[0] // block
    specs = [pl.BlockSpec((block, member.shape[1]), lambda i: (i, 0)) for member in blocked]
    specs += [
        pl.BlockSpec(member.shape, lambda i: (0, 0), pipeline_mode=pl.Buffered(1))
        for member in whole
    ]
    shapes = [jax.ShapeDtypeStruct((rows * steps, columns), kind) for rows, columns, kind in outs]
    size = sum(member.size * member.dtype.itemsize for member in (*blocked, *whole, *shapes))
    return pl.pallas_call(
        kernel,
        grid=(steps,),
        in_specs=specs,
        out_specs=[pl.BlockSpec((rows, columns), lambda i: (i, 0)) for rows, columns, _ in outs],
        out_shape=shapes,
        scratch_shapes=list(scratch),
        compiler_params=pltpu.CompilerParams(vmem_limit_bytes=60 << 20),
        cost_estimate=pl.CostEstimate(flops=flops, bytes_accessed=size, transcendentals=0),
    )(*blocked, *whole)


def layer_forward(stream, packed_w, out_w, feed, norms, head_count, block, image_rows, valid):
    rows, width = stream.shape
    units = feed[0][0].shape[1]
    outs = [
        (block, width, jnp.float32),
        (block, width, low),
        (block, 3 * width, low),
        (block, width, low),
        (block, width, jnp.float32),
        (block, width, low),
        (block, units, jnp.float32),
        (block, units, jnp.float32),
        (block, units, low),
        (block, units, low),
    ]
    return call_blocks(
        partial(layer_kernel, image_rows, valid, width // head_count),
        block,
        [stream],
        [packed_w, out_w, *feed[0], *feed[1], norms],
        outs,
        flops=2 * rows * width * (4 * width + 4 * units + 2 * block),
    )


def feed_backward(gradient, saved, feed, norms, block):
    _, normed, packed, merged, mixed, second, pre0, pre1, hidden0, hidden1 = saved
    rows, width = gradient.shape
    units = pre0.shape[1]
    grad_mixed, branch, attn, grad_pre0, grad_pre1, norm_grads = call_blocks(
        feed_kernel,
        block,
        [gradient, mixed, pre0, pre1],
        [*feed[0], *feed[1], norms],
        [
            (block, width, jnp.float32),
            (block, width, low),
            (block, width, low),
            (block, units, low),
            (block, units, low),
            (8, width, jnp.float32),
        ],
        [pltpu.VMEM((block, width), jnp.float32)],
        flops=8 * rows * width * units,
    )
    grad_down = (product_left(branch, hidden0), product_left(branch, hidden1).astype(low))
    grad_up = (product_left(second, grad_pre0), product_left(second, grad_pre1).astype(low))
    return grad_mixed, attn, grad_down, grad_up, norm_rows(norm_grads)


def attention_backward(
    grad_mixed, attn, stream, saved, packed_w, out_w, norms, head_count, block, image_rows, valid
):
    _, normed, packed, merged, mixed, second, pre0, pre1, hidden0, hidden1 = saved
    rows, width = stream.shape
    grad_x, grad_packed, norm_grads = call_blocks(
        partial(attention_kernel, image_rows, valid, width // head_count),
        block,
        [grad_mixed, attn, stream, packed],
        [packed_w, out_w, norms],
        [(block, width, jnp.float32), (block, 3 * width, low), (8, width, jnp.float32)],
        [pltpu.VMEM((block, width), low)],
        flops=2 * rows * width * (4 * width + 5 * block),
    )
    return grad_x, split_grad(normed, grad_packed), split_grad(merged, attn), norm_rows(norm_grads)


def norm_rows(partial_sums):
    sums = jnp.sum(partial_sums.reshape(-1, 8, partial_sums.shape[1]), axis=0)
    return sums[0], sums[1]


def adam_update(weight, first, second, gradient, rate):
    first = beta_one * first + (1.0 - beta_one) * gradient
    second = beta_two * second + (1.0 - beta_two) * gradient * gradient
    fix_one = 1.0 - beta_one**STEP
    fix_two = 1.0 - beta_two**STEP
    step_dir = first / fix_one / (jnp.sqrt(second / fix_two) + adam_eps)
    return (weight - rate * (step_dir + decay_rate * weight), first, second)


def own_rows(array):
    pieces = lax.axis_size(TENSOR)
    rows = array.shape[0] // pieces
    return lax.dynamic_slice_in_dim(array, lax.axis_index(TENSOR) * rows, rows, 0)


def after(value, *others):
    if not others:
        return value
    zero = sum(other[(0,) * other.ndim].astype(jnp.float32) for other in others) * 0.0
    return value + zero.astype(value.dtype)


class Links:
    def __init__(self):
        self.zero = None

    def hold(self, array):
        return array if self.zero is None else array + self.zero.astype(array.dtype)

    def round(self, *jobs):
        received = []
        for job in jobs:
            known = len(job.received)
            job.go()
            received.extend(job.received[known:])
        if received:
            corners = [other[(0,) * other.ndim].astype(jnp.float32) for other in received]
            self.zero = sum(corners) * 0.0


class Job:
    def __init__(self, steps):
        self.steps, self.result, self.ended = steps, None, False
        self.received = []

    def go(self, count=1):
        for _ in range(count):
            if self.ended:
                return
            try:
                self.received.append(next(self.steps))
            except StopIteration as stop:
                self.result, self.ended = stop.value, True

    def finish(self):
        while not self.ended:
            self.go()
        return self.result


def swap(array, axis, step):
    size = lax.axis_size(axis)
    return lax.ppermute(array, axis, [(i, i ^ step) for i in range(size)])


def halves(array):
    second = lax.axis_index("core") == 1
    half = array.shape[-1] // 2
    lower, upper = array[:, :half], array[:, half:]
    return jnp.where(second, upper, lower), jnp.where(second, lower, upper)


def join_halves(own, other):
    second = lax.axis_index("core") == 1
    return jnp.concatenate(
        [jnp.where(second, other, own), jnp.where(second, own, other)], axis=-1
    )


def gather_axis(links, array, axis, place):
    size = lax.axis_size(axis)
    step, at = size // 2, place
    while step >= 1:
        array = links.hold(jnp.expand_dims(array, at))
        other = swap(array, axis, step)
        yield other
        upper = (lax.axis_index(axis) // step) % 2 == 1
        array = jnp.concatenate(
            [jnp.where(upper, other, array), jnp.where(upper, array, other)], axis=at
        )
        at += 1
        step //= 2
    return array.reshape(array.shape[:place] + (size,) + array.shape[at:])


def gather_rows(links, piece, shard_first):
    columns = piece.shape[1:]
    if shard_first:
        whole = yield from gather_axis(links, piece, "shard", 0)
        whole = yield from gather_axis(links, whole, "heads", 1)
    else:
        whole = yield from gather_axis(links, piece, "heads", 0)
        whole = yield from gather_axis(links, whole, "shard", 0)
    return whole.reshape((-1,) + columns)


def gather_mats(links, matrices, shard_first):
    send = jnp.concatenate([halves(member)[0] for member in matrices], axis=1).astype(low)
    own = links.hold((yield from gather_rows(links, send, shard_first)))
    other = swap(own, "core", 1)
    yield other
    results, at = [], 0
    for member in matrices:
        until = at + member.shape[1] // 2
        results.append(join_halves(own[:, at:until], other[:, at:until]))
        at = until
    return results


def gather_feed(links, piece):
    whole = yield from gather_rows(links, piece, False)
    step = 1
    while step < lax.axis_size("pair"):
        whole = links.hold(whole)
        other = swap(whole, "pair", step)
        yield other
        whole = jnp.concatenate([whole, other], axis=1)
        step *= 2
    whole = links.hold(whole)
    other = swap(whole, "core", 1)
    yield other
    return [whole, other]


def reduce_axis(links, arrays, axis, place):
    size = lax.axis_size(axis)
    bits = size.bit_length() - 1
    mine = lax.axis_index(axis)
    arrays = [
        member.reshape(member.shape[:place] + (2,) * bits + member.shape[place + 1 :])
        for member in arrays
    ]
    for bit in range(bits):
        pick = partial(lax.dynamic_index_in_dim, axis=place + bits - 1 - bit, keepdims=False)
        upper = (mine >> bit) % 2
        send = [pick(member, 1 - upper).astype(low) for member in arrays]
        send = jnp.concatenate(send, axis=-1) if len(send) > 1 else send[0]
        keep = [pick(member, upper) for member in arrays]
        keep = jnp.concatenate(keep, axis=-1) if len(keep) > 1 else keep[0]
        other = swap(links.hold(send), axis, 1 << bit)
        yield other
        arrays = [keep + other.astype(jnp.float32)]
    return arrays[0]


def split_grad(left, right):
    own, other = halves(right)
    return product_left(left, own), product_left(left, other).astype(low)


def scatter_mats(links, pairs, shard_first):
    shard, heads = (lax.axis_size(axis) for axis in AXES[:2])
    others = [swap(send, "core", 1) for _, send in pairs]
    yield sum(other[:8, :128] for other in others)
    sums = [
        (own + other.astype(jnp.float32)).reshape(shard, heads, -1, own.shape[1])
        for (own, _), other in zip(pairs, others)
    ]
    if shard_first:
        total = yield from reduce_axis(links, sums, "shard", 0)
        total = yield from reduce_axis(links, [total], "heads", 0)
    else:
        total = yield from reduce_axis(links, sums, "heads", 1)
        total = yield from reduce_axis(links, [total], "shard", 0)
    step = 1
    while step < lax.axis_size("pair"):
        total = links.hold(total.astype(low))
        other = swap(total, "pair", step)
        yield other
        total = total.astype(jnp.float32) + other.astype(jnp.float32)
        step *= 2
    return total


def scatter_feed(links, own, send):
    shard, heads, pair = (lax.axis_size(axis) for axis in AXES[:3])
    other = swap(send, "core", 1)
    yield other
    total = own + other.astype(jnp.float32)
    step = pair // 2
    while step >= 1:
        half = total.shape[1] // 2
        other = swap(links.hold(total[:, half:].astype(low)), "pair", step)
        yield other
        total = total[:, :half] + other.astype(jnp.float32)
        step //= 2
    total = total.reshape(shard, heads, -1, total.shape[1])
    total = yield from reduce_axis(links, [total], "shard", 0)
    return (yield from reduce_axis(links, [total], "heads", 0))


def butterfly_sum(values):
    for axis in AXES[::-1]:
        step = 1
        while step < lax.axis_size(axis):
            values = values + swap(values, axis, step)
            step *= 2
    return values


def per_device(
    patch_pixels,
    keep_index,
    restore_index,
    masked,
    encoder_mats,
    encoder_mats_first,
    encoder_mats_second,
    decoder_mats,
    decoder_mats_first,
    decoder_mats_second,
    encoder_feed,
    encoder_feed_first,
    encoder_feed_second,
    decoder_feed,
    decoder_feed_first,
    decoder_feed_second,
    encoder_norms,
    encoder_norms_first,
    encoder_norms_second,
    decoder_norms,
    decoder_norms_first,
    decoder_norms_second,
):
    masters = (encoder_mats, decoder_mats, encoder_feed, decoder_feed, encoder_norms, decoder_norms)
    firsts = (
        encoder_mats_first,
        decoder_mats_first,
        encoder_feed_first,
        decoder_feed_first,
        encoder_norms_first,
        decoder_norms_first,
    )
    seconds = (
        encoder_mats_second,
        decoder_mats_second,
        encoder_feed_second,
        decoder_feed_second,
        encoder_norms_second,
        decoder_norms_second,
    )
    rates = (learn_rate, learn_rate, learn_rate, learn_rate, norm_rate, norm_rate)
    groups = lax.axis_size("shard") * lax.axis_size("heads")
    pieces = lax.axis_size(TENSOR)
    devices = groups * pieces

    patch_pixels = own_rows(patch_pixels)
    keep_index = own_rows(keep_index)
    restore_index = own_rows(restore_index)
    masked = own_rows(masked)
    images, patches, pixel_dim = patch_pixels.shape
    kept = keep_index.shape[1]

    enc_rows, enc_cols = encoder_mats.shape
    dec_rows, dec_cols = decoder_mats.shape
    width_enc = enc_rows * groups
    width_dec = dec_rows * groups
    enc_size, dec_size = encoder_norms.size, decoder_norms.size
    tables = jnp.concatenate([encoder_norms.reshape(-1), decoder_norms.reshape(-1)])
    tables = jnp.pad(tables, (0, -tables.size % 1024)).reshape(1, -1, 128).astype(low)
    enc_cuts = (0, width_enc, 4 * width_enc, 5 * width_enc, enc_cols)
    dec_cuts = (0, 3 * width_dec, 4 * width_dec, dec_cols)
    enc_parts = [encoder_mats[:, a:b] for a, b in zip(enc_cuts, enc_cuts[1:])]
    dec_parts = [decoder_mats[:, a:b] for a, b in zip(dec_cuts, dec_cuts[1:])]
    enc_up, enc_down = encoder_feed.astype(low)
    dec_up, dec_down = decoder_feed.astype(low)
    links = Links()
    nt = Job(gather_rows(links, tables, False))
    eh = Job(gather_mats(links, enc_parts[:2], False))
    et = Job(gather_mats(links, enc_parts[2:], True))
    eu = Job(gather_feed(links, enc_up))
    ed = Job(gather_feed(links, enc_down))
    dm = Job(gather_mats(links, dec_parts, True))
    du = Job(gather_feed(links, dec_up))
    dd = Job(gather_feed(links, dec_down))
    links.round(ed, eu, dd, du, nt, et, dm)
    links.round(ed, eu, dd, du, nt)
    links.round(eh, et, ed, dd, nt)
    links.round(ed, eh, dm, eu, du)
    links.round(eu, eh, et, dm)
    links.round(dd, du, eh, et, dm, ed, eu)
    tables = nt.finish().reshape(groups, -1)
    emb_w, enc_packed = eh.finish()
    enc_out, proj_w = et.finish()
    enc_feed = [eu.finish(), ed.finish()]
    links = Links()
    dec_packed, dec_out, pixel_w = dm.finish()
    dec_feed = [du.finish(), dd.finish()]
    enc_norm = tables[:, :enc_size].reshape(groups, -1, enc_rows).transpose(1, 0, 2)
    enc_norm = enc_norm.reshape(-1, width_enc).astype(jnp.float32)
    dec_norm = tables[:, enc_size : enc_size + dec_size].reshape(groups, -1, dec_rows)
    dec_norm = dec_norm.transpose(1, 0, 2).reshape(-1, width_dec).astype(jnp.float32)

    enc_pad = -(-kept // 64) * 64
    dec_pad = -(-patches // 16) * 16
    keep_pad = jnp.pad(keep_index, ((0, 0), (0, enc_pad - kept)), constant_values=-1)
    spots = jnp.arange(patches, dtype=jnp.int32)
    picks = (keep_pad[:, :, None] == spots).astype(low)
    picked = jnp.einsum("bkp,bpd->bkd", picks, patch_pixels, preferred_element_type=jnp.float32)
    picked = picked.astype(low).reshape(images * enc_pad, pixel_dim)
    places = jnp.asarray(positions(patches, width_enc))[jnp.maximum(keep_pad, 0)]
    enc_stream = product(picked, emb_w) + places.reshape(images * enc_pad, width_enc)
    enc_block = images * enc_pad
    enc_shape = (enc_block, enc_pad, kept)
    enc_saved = layer_forward(
        enc_stream, enc_packed, enc_out, enc_feed, enc_norm, HEADS_E, *enc_shape
    )
    enc_flat = enc_saved[0]
    enc_final = layer_norm(enc_flat, enc_norm[4], enc_norm[5]).astype(low)
    latent = product(enc_final, proj_w).reshape(images, enc_pad, width_dec)
    restore_pad = jnp.pad(
        restore_index, ((0, 0), (0, dec_pad - patches)), constant_values=enc_pad + patches
    )
    slots = jnp.arange(enc_pad, dtype=jnp.int32)
    seen = restore_pad[:, :, None] < kept
    routes = ((restore_pad[:, :, None] == slots) & seen).astype(jnp.float32)
    table = jnp.pad(positions(patches, width_dec), ((0, dec_pad - patches), (0, 0)))
    dec_stream = jnp.einsum("bpk,bkd->bpd", routes, latent, precision=lax.Precision.HIGHEST)
    dec_stream = dec_stream + jnp.where(seen, 0.0, dec_norm[6]) + table
    dec_stream = dec_stream.reshape(images * dec_pad, width_dec)
    dec_shape = (dec_pad, dec_pad, patches)
    dec_saved = layer_forward(
        dec_stream, dec_packed, dec_out, dec_feed, dec_norm, HEADS_D, *dec_shape
    )
    row_pad = ((0, 0), (0, dec_pad - patches))
    pixels = jnp.pad(patch_pixels, (*row_pad, (0, 0))).reshape(images * dec_pad, pixel_dim)
    chosen = jnp.pad(masked.astype(jnp.float32), row_pad)
    scaling = 1.0 / (images * devices * (patches - kept) * pixel_dim)
    dec_final, grad_pred, grad_stream, dec_third, losses = call_blocks(
        partial(loss_kernel, scaling),
        dec_pad,
        [dec_saved[0], pixels, chosen.reshape(images * dec_pad, 1)],
        [pixel_w, dec_norm],
        [
            (dec_pad, width_dec, low),
            (dec_pad, pixel_dim, low),
            (dec_pad, width_dec, jnp.float32),
            (8, width_dec, jnp.float32),
            (8, 128, jnp.float32),
        ],
        flops=4 * images * dec_pad * width_dec * pixel_dim,
    )
    dec_third = norm_rows(dec_third)
    loss_local = jnp.sum(losses.reshape(images, 8, 128)[:, 0, 0])
    grad_pixel_w = split_grad(dec_final, grad_pred)
    grad_mixed, attn, grad_down, grad_up, dec_second = feed_backward(
        grad_stream, dec_saved, dec_feed, dec_norm, dec_pad
    )
    dd = Job(scatter_feed(links, *grad_down))
    du = Job(scatter_feed(links, *grad_up))
    for job in (dd, du, dd, du):
        job.go()
    grad_mixed = after(grad_mixed, dd.received[0], du.received[0])
    grad_stream, grad_packed_w, grad_out_w, dec_first = attention_backward(
        grad_mixed, attn, dec_stream, dec_saved, dec_packed, dec_out, dec_norm, HEADS_D, *dec_shape
    )
    grad_stream = after(grad_stream, dd.received[1], du.received[1])
    dm = Job(scatter_mats(links, [grad_packed_w, grad_out_w, grad_pixel_w], False))
    for job in (dm, dd, du):
        job.go()

    grad_cube = grad_stream.reshape(images, dec_pad, width_dec)
    grad_latent = jnp.einsum(
        "bpk,bpd->bkd", routes, grad_cube, precision=lax.Precision.HIGHEST
    ).reshape(images * enc_pad, width_dec)
    grad_latent = grad_latent.astype(low)
    grad_mask = jnp.sum(jnp.where(seen, 0.0, grad_cube), axis=(0, 1))
    grad_proj = split_grad(enc_final, grad_latent)
    grad_final = product_right(grad_latent, proj_w)
    final_pull = jax.vjp(layer_norm, enc_flat, enc_norm[4], enc_norm[5])[1]
    grad_stream, *enc_third = final_pull(grad_final)
    grad_mixed, attn, grad_down, grad_up, enc_second = feed_backward(
        grad_stream, enc_saved, enc_feed, enc_norm, enc_block
    )
    ed = Job(scatter_feed(links, *grad_down))
    eu = Job(scatter_feed(links, *grad_up))
    for job in (ed, eu):
        job.go()
    grad_stream, grad_packed_w, grad_out_w, enc_first = attention_backward(
        grad_mixed, attn, enc_stream, enc_saved, enc_packed, enc_out, enc_norm, HEADS_E, *enc_shape
    )
    grad_embed = split_grad(picked, grad_stream.astype(low))
    et = Job(scatter_mats(links, [grad_out_w, grad_proj], True))
    eh = Job(scatter_mats(links, [grad_embed, grad_packed_w], True))
    for job in (eh, et):
        job.go()
    links.round(ed, eh, dm, dd, du)
    links.round(eu, ed, et, dm, eh)
    links.round(eu, dm, eh, et, dd, du)
    links.round(ed, eu, et, eh, dm)
    links.round(ed, eu, et)
    dec_feed_sum = (du.finish(), dd.finish())
    dec_mats_sum = dm.finish()
    enc_tail_sum = et.finish()
    enc_feed_sum = (eu.finish(), ed.finish())
    enc_head_sum = eh.finish()

    norm_grads = [
        jnp.stack([*enc_first, *enc_second, *enc_third]),
        jnp.stack([*dec_first, *dec_second, *dec_third, grad_mask]),
    ]
    copies = lax.axis_size("pair")
    squares = sum(jnp.sum(jnp.square(member)) for member in (*enc_feed_sum, *dec_feed_sum))
    squares += sum(
        jnp.sum(jnp.square(member)) for member in (enc_tail_sum, enc_head_sum, dec_mats_sum)
    ) * (1.0 / copies)
    packed = jnp.concatenate(
        [member.reshape(-1) for member in norm_grads] + [jnp.stack([loss_local, squares])]
    )
    packed = jnp.pad(packed, (0, -packed.size % 1024)).reshape(-1, 128)
    packed = butterfly_sum(packed).reshape(-1)
    enc_total, dec_total = (member.size for member in norm_grads)
    both_total = enc_total + dec_total
    loss = packed[both_total]
    total = packed[both_total + 1] + jnp.sum(jnp.square(packed[:both_total]))
    group = lax.axis_index(("shard", "heads"))
    enc_norm_sum = packed[:enc_total].reshape(-1, groups, enc_rows)
    dec_norm_sum = packed[enc_total : enc_total + dec_total].reshape(-1, groups, dec_rows)
    enc_norm_sum = lax.dynamic_index_in_dim(enc_norm_sum, group, 1, keepdims=False)
    dec_norm_sum = lax.dynamic_index_in_dim(dec_norm_sum, group, 1, keepdims=False)

    def whole_columns(own, parts):
        own = after(own, enc_head_sum, enc_tail_sum)
        other = swap(own, "core", 1)
        results, at = [], 0
        for member in parts:
            until = at + member.shape[1] // 2
            results.append(join_halves(own[:, at:until], other[:, at:until]))
            at = until
        return results

    reduced = (
        jnp.concatenate(
            whole_columns(enc_head_sum, enc_parts[:2]) + whole_columns(enc_tail_sum, enc_parts[2:]),
            axis=1,
        ),
        jnp.concatenate(whole_columns(dec_mats_sum, dec_parts), axis=1),
        jnp.stack(enc_feed_sum),
        jnp.stack(dec_feed_sum),
        enc_norm_sum,
        dec_norm_sum,
    )
    norm = jnp.sqrt(total)
    factor = clip_limit / jnp.maximum(norm, clip_limit)
    results = [loss, norm]
    for weight, first, second, gradient, rate in zip(masters, firsts, seconds, reduced, rates):
        results.extend(adam_update(weight, first, second, gradient * factor, rate))
    return tuple(results)


def solution(mesh):
    shard, heads, tensor = (mesh.shape[axis] for axis in ("shard", "heads", "tensor"))
    mesh = Mesh(mesh.devices.reshape(shard, heads, tensor // 2, 2), AXES)
    rows = P(("shard", "heads"), None)
    feeds = P(None, ("shard", "heads"), TENSOR)
    norms = P(None, ("shard", "heads"))
    states = (rows,) * 6 + (feeds,) * 6 + (norms,) * 6
    return jax.shard_map(
        per_device,
        mesh=mesh,
        in_specs=(P(("shard", "heads"), None, None), rows, rows, rows) + states,
        out_specs=(P(), P()) + states,
        check_vma=False,
    )
```

```python
from functools import partial
import math

import jax
import jax.numpy as jnp
import numpy as np
from jax import lax
from jax.experimental import pallas as pl
from jax.experimental.pallas import tpu as pltpu
from jax.sharding import Mesh, PartitionSpec as P

HEADS_E = 12
HEADS_D = 16
STEP = 5

clip_limit = 0.01
beta_one = 0.9
beta_two = 0.999
learn_rate = 0.05
norm_rate = 0.5
decay_rate = 0.05
adam_eps = 1e-08
norm_eps = 1e-06

AXES = ("shard", "heads", "pair", "core")
TENSOR = ("pair", "core")
low = jnp.bfloat16


def positions(places, features):
    where = np.arange(places, dtype=np.float32)[:, None]
    column = np.arange(features // 2, dtype=np.float32)[None, :]
    angles = where * np.exp(column * np.float32(-2.0 * math.log(10000.0) / features))
    return np.concatenate([np.sin(angles), np.cos(angles)], axis=1).astype(np.float32)


def layer_norm(rows, gain, shift):
    centered = rows - jnp.mean(rows, axis=-1, keepdims=True)
    spread = jnp.mean(centered * centered, axis=-1, keepdims=True)
    return centered * lax.rsqrt(spread + norm_eps) * gain + shift


def product(left, right):
    return jnp.dot(left, right, preferred_element_type=jnp.float32)


def product_left(left, right):
    return lax.dot_general(
        left, right, (((0,), (0,)), ((), ())), preferred_element_type=jnp.float32
    )


def product_right(left, right):
    return lax.dot_general(
        left, right, (((1,), (1,)), ((), ())), preferred_element_type=jnp.float32
    )


def norm_forward(rows, gain, shift):
    centered = rows - jnp.mean(rows, axis=-1, keepdims=True)
    scale = lax.rsqrt(jnp.mean(centered * centered, axis=-1, keepdims=True) + norm_eps)
    return centered * scale * gain + shift


def norm_backward(rows, gain, gradient):
    centered = rows - jnp.mean(rows, axis=-1, keepdims=True)
    scale = lax.rsqrt(jnp.mean(centered * centered, axis=-1, keepdims=True) + norm_eps)
    unit = centered * scale
    inner = gradient * gain
    back = inner - jnp.mean(inner, axis=-1, keepdims=True)
    back = (back - unit * jnp.mean(inner * unit, axis=-1, keepdims=True)) * scale
    gains = jnp.sum(gradient * unit, axis=0, keepdims=True)
    return back, gains, jnp.sum(gradient, axis=0, keepdims=True)


def key_mask(rows, image_rows, valid):
    row = lax.broadcasted_iota(jnp.int32, (rows, rows), 0)
    column = lax.broadcasted_iota(jnp.int32, (rows, rows), 1)
    if rows == image_rows:
        return column < valid
    mask = None
    for start in range(0, rows, image_rows):
        inside = (row >= start) & (row < start + image_rows)
        inside = inside & (column >= start) & (column < start + valid)
        mask = inside if mask is None else mask | inside
    return mask


def head_lanes(rows, head_size):
    lane = lax.broadcasted_iota(jnp.int32, (rows, 128), 1)
    return [
        jnp.where((lane >= start) & (lane < start + head_size), 1.0, 0.0).astype(low)
        for start in range(0, 128, head_size)
    ]


def softmax_rows(queries, key_rows, mask, score_scale):
    scores = product_right(queries, key_rows) * score_scale
    scores = jnp.where(mask, scores, -1e30)
    powers = jnp.exp(scores - jnp.max(scores, axis=-1, keepdims=True))
    return powers * (1.0 / jnp.sum(powers, axis=-1, keepdims=True))


def chunk_of(size):
    return 512 if size % 512 == 0 else 256 if size % 256 == 0 else size


def layer_kernel(
    image_rows, valid, head_size, x, packed_w, out_w, up0, up1, down0, down1, norms,
    result, normed, packed, merged, mixed, second, pre0, pre1, hidden0, hidden1,
):
    rows, width = x.shape
    normed[...] = norm_forward(x[...], norms[0:1, :], norms[1:2, :]).astype(low)

    @pl.loop(0, 3)
    def _(part):
        columns = pl.ds(pl.multiple_of(part * width, 128), width)
        packed[:, columns] = product(normed[...], packed_w[:, columns]).astype(low)

    @pl.loop(0, width // 128)
    def _(group):
        mask = key_mask(rows, image_rows, valid)
        base = group * 128
        queries, key_rows, value_rows = (
            packed[:, pl.ds(pl.multiple_of(part * width + base, 128), 128)] for part in range(3)
        )
        total = jnp.zeros((rows, 128), jnp.float32)
        for lanes in head_lanes(rows, head_size):
            shares = softmax_rows(queries * lanes, key_rows, mask, head_size ** (-0.5))
            total = total + product(shares.astype(low), value_rows * lanes)
        merged[:, pl.ds(pl.multiple_of(base, 128), 128)] = total.astype(low)

    mixed[...] = x[...] + product(merged[...], out_w[...])
    second[...] = norm_forward(mixed[...], norms[2:3, :], norms[3:4, :]).astype(low)
    result[...] = mixed[...]
    for up, down, pre, hidden in ((up0, down0, pre0, hidden0), (up1, down1, pre1, hidden1)):
        size = chunk_of(up.shape[1])

        @pl.loop(0, up.shape[1] // size)
        def _(part):
            columns = pl.ds(pl.multiple_of(part * size, 128), size)
            value = product(second[...], up[:, columns])
            pre[:, columns] = value
            half = 0.5 * (1.0 + lax.erf(value * math.sqrt(0.5)))
            units = (value * half).astype(low)
            hidden[:, columns] = units
            result[...] += product_right(units, down[:, columns])


def feed_kernel(
    gradient, mixed, pre0, pre1, up0, up1, down0, down1, norms,
    grad_mixed, branch, attn, grad_pre0, grad_pre1, norm_grads, total,
):
    branch[...] = gradient[...].astype(low)
    total[...] = jnp.zeros_like(total)
    for up, down, pre, grad_pre in ((up0, down0, pre0, grad_pre0), (up1, down1, pre1, grad_pre1)):
        size = chunk_of(up.shape[1])

        @pl.loop(0, up.shape[1] // size)
        def _(part):
            columns = pl.ds(pl.multiple_of(part * size, 128), size)
            value = pre[:, columns]
            slope = 0.5 * (1.0 + lax.erf(value * math.sqrt(0.5)))
            slope += value * jnp.exp(-0.5 * value * value) * (1.0 / math.sqrt(2.0 * math.pi))
            units = (product(branch[...], down[:, columns]) * slope).astype(low)
            grad_pre[:, columns] = units
            total[...] += product_right(units, up[:, columns])

    back, gains, shifts = norm_backward(mixed[...], norms[2:3, :], total[...])
    back = back + gradient[...]
    grad_mixed[...] = back
    attn[...] = back.astype(low)
    norm_grads[0:1, :] = gains
    norm_grads[1:2, :] = shifts


def attention_kernel(
    image_rows, valid, head_size, grad_mixed, attn, x, packed, packed_w, out_w, norms,
    grad_x, grad_packed, norm_grads, grad_merged,
):
    rows, width = x.shape
    score_scale = head_size ** (-0.5)
    grad_merged[...] = product_right(attn[...], out_w[...]).astype(low)

    @pl.loop(0, width // 128)
    def _(group):
        mask = key_mask(rows, image_rows, valid)
        base = group * 128
        places = [pl.ds(pl.multiple_of(part * width + base, 128), 128) for part in range(3)]
        queries, key_rows, value_rows = (packed[:, place] for place in places)
        grad_out = grad_merged[:, pl.ds(pl.multiple_of(base, 128), 128)]
        totals = [jnp.zeros((rows, 128), jnp.float32)] * 3
        for lanes in head_lanes(rows, head_size):
            own_queries, own_out = queries * lanes, grad_out * lanes
            shares = softmax_rows(own_queries, key_rows, mask, score_scale)
            grad_shares = product_right(own_out, value_rows)
            inner = jnp.sum(shares * grad_shares, axis=-1, keepdims=True)
            grad_scores = (shares * (grad_shares - inner)).astype(low)
            totals = [
                totals[0] + product(grad_scores, key_rows * lanes),
                totals[1] + product_left(grad_scores, own_queries),
                totals[2] + product_left(shares.astype(low), own_out),
            ]
        scales = (score_scale, score_scale, 1.0)
        for place, total, scale in zip(places, totals, scales):
            grad_packed[:, place] = (total * scale).astype(low)

    grad_normed = product_right(grad_packed[...], packed_w[...])
    back, gains, shifts = norm_backward(x[...], norms[0:1, :], grad_normed)
    grad_x[...] = back + grad_mixed[...]
    norm_grads[0:1, :] = gains
    norm_grads[1:2, :] = shifts


def loss_kernel(
    scaling, x, pixels, chosen, pixel_w, norms, final, grad_pred, grad_x, norm_grads, loss
):
    final[...] = norm_forward(x[...], norms[4:5, :], norms[5:6, :]).astype(low)
    errors = product(final[...], pixel_w[...]) - pixels[...].astype(jnp.float32)
    errors = errors * chosen[...]
    loss[...] = jnp.broadcast_to(jnp.sum(errors * errors) * scaling, loss.shape)
    grad_pred[...] = (errors * (2.0 * scaling)).astype(low)
    grad_final = product_right(grad_pred[...], pixel_w[...])
    back, gains, shifts = norm_backward(x[...], norms[4:5, :], grad_final)
    grad_x[...] = back
    norm_grads[0:1, :] = gains
    norm_grads[1:2, :] = shifts


def call_blocks(kernel, block, blocked, whole, outs, scratch=(), flops=0):
    steps = blocked[0].shape[0] // block
    specs = [pl.BlockSpec((block, member.shape[1]), lambda i: (i, 0)) for member in blocked]
    specs += [
        pl.BlockSpec(member.shape, lambda i: (0, 0), pipeline_mode=pl.Buffered(1))
        for member in whole
    ]
    shapes = [jax.ShapeDtypeStruct((rows * steps, columns), kind) for rows, columns, kind in outs]
    size = sum(member.size * member.dtype.itemsize for member in (*blocked, *whole, *shapes))
    return pl.pallas_call(
        kernel,
        grid=(steps,),
        in_specs=specs,
        out_specs=[pl.BlockSpec((rows, columns), lambda i: (i, 0)) for rows, columns, _ in outs],
        out_shape=shapes,
        scratch_shapes=list(scratch),
        compiler_params=pltpu.CompilerParams(vmem_limit_bytes=60 << 20),
        cost_estimate=pl.CostEstimate(flops=flops, bytes_accessed=size, transcendentals=0),
    )(*blocked, *whole)


def layer_forward(stream, packed_w, out_w, feed, norms, head_count, block, image_rows, valid):
    rows, width = stream.shape
    units = feed[0][0].shape[1]
    outs = [
        (block, width, jnp.float32),
        (block, width, low),
        (block, 3 * width, low),
        (block, width, low),
        (block, width, jnp.float32),
        (block, width, low),
        (block, units, jnp.float32),
        (block, units, jnp.float32),
        (block, units, low),
        (block, units, low),
    ]
    return call_blocks(
        partial(layer_kernel, image_rows, valid, width // head_count),
        block,
        [stream],
        [packed_w, out_w, *feed[0], *feed[1], norms],
        outs,
        flops=2 * rows * width * (4 * width + 4 * units + 2 * block),
    )


def feed_backward(gradient, saved, feed, norms, block):
    _, normed, packed, merged, mixed, second, pre0, pre1, hidden0, hidden1 = saved
    rows, width = gradient.shape
    units = pre0.shape[1]
    grad_mixed, branch, attn, grad_pre0, grad_pre1, norm_grads = call_blocks(
        feed_kernel,
        block,
        [gradient, mixed, pre0, pre1],
        [*feed[0], *feed[1], norms],
        [
            (block, width, jnp.float32),
            (block, width, low),
            (block, width, low),
            (block, units, low),
            (block, units, low),
            (8, width, jnp.float32),
        ],
        [pltpu.VMEM((block, width), jnp.float32)],
        flops=8 * rows * width * units,
    )
    grad_down = (product_left(branch, hidden0), product_left(branch, hidden1).astype(low))
    grad_up = (product_left(second, grad_pre0), product_left(second, grad_pre1).astype(low))
    return grad_mixed, attn, grad_down, grad_up, norm_rows(norm_grads)


def attention_backward(
    grad_mixed, attn, stream, saved, packed_w, out_w, norms, head_count, block, image_rows, valid
):
    _, normed, packed, merged, mixed, second, pre0, pre1, hidden0, hidden1 = saved
    rows, width = stream.shape
    grad_x, grad_packed, norm_grads = call_blocks(
        partial(attention_kernel, image_rows, valid, width // head_count),
        block,
        [grad_mixed, attn, stream, packed],
        [packed_w, out_w, norms],
        [(block, width, jnp.float32), (block, 3 * width, low), (8, width, jnp.float32)],
        [pltpu.VMEM((block, width), low)],
        flops=2 * rows * width * (4 * width + 5 * block),
    )
    return grad_x, split_grad(normed, grad_packed), split_grad(merged, attn), norm_rows(norm_grads)


def norm_rows(partial_sums):
    sums = jnp.sum(partial_sums.reshape(-1, 8, partial_sums.shape[1]), axis=0)
    return sums[0], sums[1]


def adam_update(weight, first, second, gradient, rate):
    first = beta_one * first + (1.0 - beta_one) * gradient
    second = beta_two * second + (1.0 - beta_two) * gradient * gradient
    fix_one = 1.0 - beta_one**STEP
    fix_two = 1.0 - beta_two**STEP
    step_dir = first / fix_one / (jnp.sqrt(second / fix_two) + adam_eps)
    return (weight - rate * (step_dir + decay_rate * weight), first, second)


def own_rows(array):
    pieces = lax.axis_size(TENSOR)
    rows = array.shape[0] // pieces
    return lax.dynamic_slice_in_dim(array, lax.axis_index(TENSOR) * rows, rows, 0)


def after(value, *others):
    if not others:
        return value
    zero = sum(other[(0,) * other.ndim].astype(jnp.float32) for other in others) * 0.0
    return value + zero.astype(value.dtype)


class Links:
    def __init__(self):
        self.zero = None

    def swap(self, array, axis, step):
        if self.zero is not None:
            array = array + self.zero.astype(array.dtype)
        return swap(array, axis, step)

    def round(self, *jobs):
        received = []
        for job in jobs:
            known = len(job.received)
            job.go()
            received.extend(job.received[known:])
        corners = [other[(0,) * other.ndim].astype(jnp.float32) for other in received]
        self.zero = sum(corners) * 0.0


class Job:
    def __init__(self, steps):
        self.steps, self.result, self.ended = steps, None, False
        self.received = []

    def go(self, count=1):
        for _ in range(count):
            if self.ended:
                return
            try:
                self.received.append(next(self.steps))
            except StopIteration as stop:
                self.result, self.ended = stop.value, True

    def finish(self):
        while not self.ended:
            self.go()
        return self.result


def swap(array, axis, step):
    size = lax.axis_size(axis)
    return lax.ppermute(array, axis, [(i, i ^ step) for i in range(size)])


def halves(array):
    second = lax.axis_index("core") == 1
    half = array.shape[-1] // 2
    lower, upper = array[:, :half], array[:, half:]
    return jnp.where(second, upper, lower), jnp.where(second, lower, upper)


def join_halves(own, other):
    second = lax.axis_index("core") == 1
    return jnp.concatenate(
        [jnp.where(second, other, own), jnp.where(second, own, other)], axis=-1
    )


def gather_axis(links, array, axis, place):
    size = lax.axis_size(axis)
    step, at = size // 2, place
    while step >= 1:
        array = jnp.expand_dims(array, at)
        other = links.swap(array, axis, step)
        yield other
        upper = (lax.axis_index(axis) // step) % 2 == 1
        array = jnp.concatenate(
            [jnp.where(upper, other, array), jnp.where(upper, array, other)], axis=at
        )
        at += 1
        step //= 2
    return array.reshape(array.shape[:place] + (size,) + array.shape[at:])


def gather_rows(links, piece, shard_first=False):
    columns = piece.shape[1:]
    if shard_first:
        whole = yield from gather_axis(links, piece, "shard", 0)
        whole = yield from gather_axis(links, whole, "heads", 1)
    else:
        whole = yield from gather_axis(links, piece, "heads", 0)
        whole = yield from gather_axis(links, whole, "shard", 0)
    return whole.reshape((-1,) + columns)


def gather_mats(links, matrices):
    send = jnp.concatenate([halves(member)[0] for member in matrices], axis=1).astype(low)
    own = yield from gather_rows(links, send)
    other = links.swap(own, "core", 1)
    yield other
    results, at = [], 0
    for member in matrices:
        until = at + member.shape[1] // 2
        results.append(join_halves(own[:, at:until], other[:, at:until]))
        at = until
    return results


def gather_feed(links, piece, shard_first):
    whole = yield from gather_rows(links, piece, shard_first)
    step = 1
    while step < lax.axis_size("pair"):
        other = links.swap(whole, "pair", step)
        yield other
        whole = jnp.concatenate([whole, other], axis=1)
        step *= 2
    other = links.swap(whole, "core", 1)
    yield other
    return [whole, other]


def reduce_axis(links, arrays, axis, place):
    size = lax.axis_size(axis)
    bits = size.bit_length() - 1
    mine = lax.axis_index(axis)
    arrays = [
        member.reshape(member.shape[:place] + (2,) * bits + member.shape[place + 1 :])
        for member in arrays
    ]
    for bit in range(bits):
        pick = partial(lax.dynamic_index_in_dim, axis=place + bits - 1 - bit, keepdims=False)
        upper = (mine >> bit) % 2
        send = [pick(member, 1 - upper).astype(low) for member in arrays]
        send = jnp.concatenate(send, axis=-1) if len(send) > 1 else send[0]
        keep = [pick(member, upper) for member in arrays]
        keep = jnp.concatenate(keep, axis=-1) if len(keep) > 1 else keep[0]
        other = links.swap(send, axis, 1 << bit)
        yield other
        arrays = [keep + other.astype(jnp.float32)]
    return arrays[0]


def split_grad(left, right):
    own, other = halves(right)
    return product_left(left, own), product_left(left, other).astype(low)


def scatter_mats(links, pairs, shard_first):
    shard, heads = (lax.axis_size(axis) for axis in AXES[:2])
    others = [links.swap(send, "core", 1) for _, send in pairs]
    yield sum(other[:8, :128] for other in others)
    sums = [
        (own + other.astype(jnp.float32)).reshape(shard, heads, -1, own.shape[1])
        for (own, _), other in zip(pairs, others)
    ]
    if shard_first:
        total = yield from reduce_axis(links, sums, "shard", 0)
        total = yield from reduce_axis(links, [total], "heads", 0)
    else:
        total = yield from reduce_axis(links, sums, "heads", 1)
        total = yield from reduce_axis(links, [total], "shard", 0)
    step = 1
    while step < lax.axis_size("pair"):
        total = total.astype(low)
        other = links.swap(total, "pair", step)
        yield other
        total = total.astype(jnp.float32) + other.astype(jnp.float32)
        step *= 2
    return total


def scatter_feed(links, own, send):
    shard, heads, pair = (lax.axis_size(axis) for axis in AXES[:3])
    other = links.swap(send, "core", 1)
    yield other
    total = own + other.astype(jnp.float32)
    step = pair // 2
    while step >= 1:
        half = total.shape[1] // 2
        other = links.swap(total[:, half:].astype(low), "pair", step)
        yield other
        total = total[:, :half] + other.astype(jnp.float32)
        step //= 2
    total = total.reshape(shard, heads, -1, total.shape[1])
    total = yield from reduce_axis(links, [total], "shard", 0)
    return (yield from reduce_axis(links, [total], "heads", 0))


def butterfly_sum(values):
    for axis in AXES[::-1]:
        step = 1
        while step < lax.axis_size(axis):
            values = values + swap(values, axis, step)
            step *= 2
    return values


def per_device(
    patch_pixels,
    keep_index,
    restore_index,
    masked,
    encoder_mats,
    encoder_mats_first,
    encoder_mats_second,
    decoder_mats,
    decoder_mats_first,
    decoder_mats_second,
    encoder_feed,
    encoder_feed_first,
    encoder_feed_second,
    decoder_feed,
    decoder_feed_first,
    decoder_feed_second,
    encoder_norms,
    encoder_norms_first,
    encoder_norms_second,
    decoder_norms,
    decoder_norms_first,
    decoder_norms_second,
):
    masters = (encoder_mats, decoder_mats, encoder_feed, decoder_feed, encoder_norms, decoder_norms)
    firsts = (
        encoder_mats_first,
        decoder_mats_first,
        encoder_feed_first,
        decoder_feed_first,
        encoder_norms_first,
        decoder_norms_first,
    )
    seconds = (
        encoder_mats_second,
        decoder_mats_second,
        encoder_feed_second,
        decoder_feed_second,
        encoder_norms_second,
        decoder_norms_second,
    )
    rates = (learn_rate, learn_rate, learn_rate, learn_rate, norm_rate, norm_rate)
    groups = lax.axis_size("shard") * lax.axis_size("heads")
    pieces = lax.axis_size(TENSOR)
    devices = groups * pieces

    patch_pixels = own_rows(patch_pixels)
    keep_index = own_rows(keep_index)
    restore_index = own_rows(restore_index)
    masked = own_rows(masked)
    images, patches, pixel_dim = patch_pixels.shape
    kept = keep_index.shape[1]

    enc_rows, enc_cols = encoder_mats.shape
    dec_rows, dec_cols = decoder_mats.shape
    width_enc = enc_rows * groups
    width_dec = dec_rows * groups
    enc_size, dec_size = encoder_norms.size, decoder_norms.size
    tables = jnp.concatenate([encoder_norms.reshape(-1), decoder_norms.reshape(-1)])
    tables = jnp.pad(tables, (0, -tables.size % 1024)).reshape(1, -1, 128).astype(low)
    links = Links()
    tables = Job(gather_rows(Links(), tables)).finish().reshape(groups, -1)
    enc_norm = tables[:, :enc_size].reshape(groups, -1, enc_rows).transpose(1, 0, 2)
    enc_norm = enc_norm.reshape(-1, width_enc).astype(jnp.float32)
    dec_norm = tables[:, enc_size : enc_size + dec_size].reshape(groups, -1, dec_rows)
    dec_norm = dec_norm.transpose(1, 0, 2).reshape(-1, width_dec).astype(jnp.float32)

    enc_cuts = (0, width_enc, 4 * width_enc, 5 * width_enc, enc_cols)
    dec_cuts = (0, 3 * width_dec, 4 * width_dec, dec_cols)
    enc_parts = [encoder_mats[:, a:b] for a, b in zip(enc_cuts, enc_cuts[1:])]
    dec_parts = [decoder_mats[:, a:b] for a, b in zip(dec_cuts, dec_cuts[1:])]
    enc_up, enc_down = encoder_feed.astype(low)
    dec_up, dec_down = decoder_feed.astype(low)
    eh = Job(gather_mats(links, enc_parts[:2]))
    et = Job(gather_mats(links, enc_parts[2:]))
    eu = Job(gather_feed(links, enc_up, False))
    ed = Job(gather_feed(links, enc_down, True))
    dm = Job(gather_mats(links, dec_parts))
    du = Job(gather_feed(links, dec_up, False))
    dd = Job(gather_feed(links, dec_down, True))
    for job in (eh, ed, et, dd, eh, ed, et, eu, eh, ed, eu, et, dd, eu, ed, dm, dd, eu):
        job.go()
    for job in (dm, du, dd, dm, du, du, du):
        job.go()
    emb_w, enc_packed = eh.finish()
    enc_out, proj_w = et.finish()
    enc_feed = [eu.finish(), ed.finish()]
    dec_packed, dec_out, pixel_w = dm.finish()
    dec_feed = [du.finish(), dd.finish()]

    enc_pad = -(-kept // 64) * 64
    dec_pad = -(-patches // 16) * 16
    keep_pad = jnp.pad(keep_index, ((0, 0), (0, enc_pad - kept)), constant_values=-1)
    spots = jnp.arange(patches, dtype=jnp.int32)
    picks = (keep_pad[:, :, None] == spots).astype(low)
    picked = jnp.einsum("bkp,bpd->bkd", picks, patch_pixels, preferred_element_type=jnp.float32)
    picked = picked.astype(low).reshape(images * enc_pad, pixel_dim)
    places = jnp.asarray(positions(patches, width_enc))[jnp.maximum(keep_pad, 0)]
    enc_stream = product(picked, emb_w) + places.reshape(images * enc_pad, width_enc)
    enc_block = images * enc_pad
    enc_shape = (enc_block, enc_pad, kept)
    enc_saved = layer_forward(
        enc_stream, enc_packed, enc_out, enc_feed, enc_norm, HEADS_E, *enc_shape
    )
    enc_flat = enc_saved[0]
    enc_final = layer_norm(enc_flat, enc_norm[4], enc_norm[5]).astype(low)
    latent = product(enc_final, proj_w).reshape(images, enc_pad, width_dec)
    restore_pad = jnp.pad(
        restore_index, ((0, 0), (0, dec_pad - patches)), constant_values=enc_pad + patches
    )
    slots = jnp.arange(enc_pad, dtype=jnp.int32)
    seen = restore_pad[:, :, None] < kept
    routes = ((restore_pad[:, :, None] == slots) & seen).astype(jnp.float32)
    table = jnp.pad(positions(patches, width_dec), ((0, dec_pad - patches), (0, 0)))
    dec_stream = jnp.einsum("bpk,bkd->bpd", routes, latent, precision=lax.Precision.HIGHEST)
    dec_stream = dec_stream + jnp.where(seen, 0.0, dec_norm[6]) + table
    dec_stream = dec_stream.reshape(images * dec_pad, width_dec)
    dec_shape = (dec_pad, dec_pad, patches)
    dec_saved = layer_forward(
        dec_stream, dec_packed, dec_out, dec_feed, dec_norm, HEADS_D, *dec_shape
    )
    row_pad = ((0, 0), (0, dec_pad - patches))
    pixels = jnp.pad(patch_pixels, (*row_pad, (0, 0))).reshape(images * dec_pad, pixel_dim)
    chosen = jnp.pad(masked.astype(jnp.float32), row_pad)
    scaling = 1.0 / (images * devices * (patches - kept) * pixel_dim)
    dec_final, grad_pred, grad_stream, dec_third, losses = call_blocks(
        partial(loss_kernel, scaling),
        dec_pad,
        [dec_saved[0], pixels, chosen.reshape(images * dec_pad, 1)],
        [pixel_w, dec_norm],
        [
            (dec_pad, width_dec, low),
            (dec_pad, pixel_dim, low),
            (dec_pad, width_dec, jnp.float32),
            (8, width_dec, jnp.float32),
            (8, 128, jnp.float32),
        ],
        flops=4 * images * dec_pad * width_dec * pixel_dim,
    )
    dec_third = norm_rows(dec_third)
    loss_local = jnp.sum(losses.reshape(images, 8, 128)[:, 0, 0])
    grad_pixel_w = split_grad(dec_final, grad_pred)
    grad_mixed, attn, grad_down, grad_up, dec_second = feed_backward(
        grad_stream, dec_saved, dec_feed, dec_norm, dec_pad
    )
    dd = Job(scatter_feed(links, *grad_down))
    du = Job(scatter_feed(links, *grad_up))
    for job in (dd, du):
        job.go()
    grad_stream, grad_packed_w, grad_out_w, dec_first = attention_backward(
        grad_mixed, attn, dec_stream, dec_saved, dec_packed, dec_out, dec_norm, HEADS_D, *dec_shape
    )
    dm = Job(scatter_mats(links, [grad_packed_w, grad_out_w, grad_pixel_w], False))
    dm.go()

    grad_cube = grad_stream.reshape(images, dec_pad, width_dec)
    grad_latent = jnp.einsum(
        "bpk,bpd->bkd", routes, grad_cube, precision=lax.Precision.HIGHEST
    ).reshape(images * enc_pad, width_dec)
    grad_latent = grad_latent.astype(low)
    grad_mask = jnp.sum(jnp.where(seen, 0.0, grad_cube), axis=(0, 1))
    grad_proj = split_grad(enc_final, grad_latent)
    grad_final = product_right(grad_latent, proj_w)
    final_pull = jax.vjp(layer_norm, enc_flat, enc_norm[4], enc_norm[5])[1]
    grad_stream, *enc_third = final_pull(grad_final)
    grad_mixed, attn, grad_down, grad_up, enc_second = feed_backward(
        grad_stream, enc_saved, enc_feed, enc_norm, enc_block
    )
    ed = Job(scatter_feed(links, *grad_down))
    eu = Job(scatter_feed(links, *grad_up))
    for job in (ed, eu):
        job.go()
    grad_stream, grad_packed_w, grad_out_w, enc_first = attention_backward(
        grad_mixed, attn, enc_stream, enc_saved, enc_packed, enc_out, enc_norm, HEADS_E, *enc_shape
    )
    grad_embed = split_grad(picked, grad_stream.astype(low))
    et = Job(scatter_mats(links, [grad_out_w, grad_proj], True))
    eh = Job(scatter_mats(links, [grad_embed, grad_packed_w], True))
    for job in (eh, et):
        job.go()
    links.round(ed, eh, dm)
    links.round(eu, ed, et, dm, eh)
    links.round(dd, du, eu, dm, eh, et, ed)
    links.round(eh, dm, dd, du, eu, et, ed)
    links.zero = None
    dec_feed_sum = (du.finish(), dd.finish())
    dec_mats_sum = dm.finish()
    enc_tail_sum = et.finish()
    enc_feed_sum = (eu.finish(), ed.finish())
    enc_head_sum = eh.finish()

    norm_grads = [
        jnp.stack([*enc_first, *enc_second, *enc_third]),
        jnp.stack([*dec_first, *dec_second, *dec_third, grad_mask]),
    ]
    copies = lax.axis_size("pair")
    squares = sum(jnp.sum(jnp.square(member)) for member in (*enc_feed_sum, *dec_feed_sum))
    squares += sum(
        jnp.sum(jnp.square(member)) for member in (enc_tail_sum, enc_head_sum, dec_mats_sum)
    ) * (1.0 / copies)
    packed = jnp.concatenate(
        [member.reshape(-1) for member in norm_grads] + [jnp.stack([loss_local, squares])]
    )
    packed = jnp.pad(packed, (0, -packed.size % 1024)).reshape(-1, 128)
    packed = butterfly_sum(packed).reshape(-1)
    enc_total, dec_total = (member.size for member in norm_grads)
    both_total = enc_total + dec_total
    loss = packed[both_total]
    total = packed[both_total + 1] + jnp.sum(jnp.square(packed[:both_total]))
    group = lax.axis_index(("shard", "heads"))
    enc_norm_sum = packed[:enc_total].reshape(-1, groups, enc_rows)
    dec_norm_sum = packed[enc_total : enc_total + dec_total].reshape(-1, groups, dec_rows)
    enc_norm_sum = lax.dynamic_index_in_dim(enc_norm_sum, group, 1, keepdims=False)
    dec_norm_sum = lax.dynamic_index_in_dim(dec_norm_sum, group, 1, keepdims=False)

    def whole_columns(own, parts):
        own = after(own, enc_head_sum, enc_tail_sum)
        other = swap(own, "core", 1)
        results, at = [], 0
        for member in parts:
            until = at + member.shape[1] // 2
            results.append(join_halves(own[:, at:until], other[:, at:until]))
            at = until
        return results

    reduced = (
        jnp.concatenate(
            whole_columns(enc_head_sum, enc_parts[:2]) + whole_columns(enc_tail_sum, enc_parts[2:]),
            axis=1,
        ),
        jnp.concatenate(whole_columns(dec_mats_sum, dec_parts), axis=1),
        jnp.stack(enc_feed_sum),
        jnp.stack(dec_feed_sum),
        enc_norm_sum,
        dec_norm_sum,
    )
    norm = jnp.sqrt(total)
    factor = clip_limit / jnp.maximum(norm, clip_limit)
    results = [loss, norm]
    for weight, first, second, gradient, rate in zip(masters, firsts, seconds, reduced, rates):
        results.extend(adam_update(weight, first, second, gradient * factor, rate))
    return tuple(results)


def solution(mesh):
    shard, heads, tensor = (mesh.shape[axis] for axis in ("shard", "heads", "tensor"))
    mesh = Mesh(mesh.devices.reshape(shard, heads, tensor // 2, 2), AXES)
    rows = P(("shard", "heads"), None)
    feeds = P(None, ("shard", "heads"), TENSOR)
    norms = P(None, ("shard", "heads"))
    states = (rows,) * 6 + (feeds,) * 6 + (norms,) * 6
    return jax.shard_map(
        per_device,
        mesh=mesh,
        in_specs=(P(("shard", "heads"), None, None), rows, rows, rows) + states,
        out_specs=(P(), P()) + states,
        check_vma=False,
    )
```

```python
from functools import partial
import math

import jax
import jax.numpy as jnp
import numpy as np
from jax import lax
from jax.experimental import pallas as pl
from jax.experimental.pallas import tpu as pltpu
from jax.sharding import Mesh, PartitionSpec as P

HEADS_E = 12
HEADS_D = 16
STEP = 5

clip_limit = 0.01
beta_one = 0.9
beta_two = 0.999
learn_rate = 0.05
norm_rate = 0.5
decay_rate = 0.05
adam_eps = 1e-08
norm_eps = 1e-06

AXES = ("shard", "heads", "pair", "core")
TENSOR = ("pair", "core")
low = jnp.bfloat16


def positions(places, features):
    where = np.arange(places, dtype=np.float32)[:, None]
    column = np.arange(features // 2, dtype=np.float32)[None, :]
    angles = where * np.exp(column * np.float32(-2.0 * math.log(10000.0) / features))
    return np.concatenate([np.sin(angles), np.cos(angles)], axis=1).astype(np.float32)


def layer_norm(rows, gain, shift):
    centered = rows - jnp.mean(rows, axis=-1, keepdims=True)
    spread = jnp.mean(centered * centered, axis=-1, keepdims=True)
    return centered * lax.rsqrt(spread + norm_eps) * gain + shift


def product(left, right):
    return jnp.dot(left, right, preferred_element_type=jnp.float32)


def product_left(left, right):
    return lax.dot_general(
        left, right, (((0,), (0,)), ((), ())), preferred_element_type=jnp.float32
    )


def product_right(left, right):
    return lax.dot_general(
        left, right, (((1,), (1,)), ((), ())), preferred_element_type=jnp.float32
    )


def norm_forward(rows, gain, shift):
    centered = rows - jnp.mean(rows, axis=-1, keepdims=True)
    scale = lax.rsqrt(jnp.mean(centered * centered, axis=-1, keepdims=True) + norm_eps)
    return centered * scale * gain + shift


def norm_backward(rows, gain, gradient):
    centered = rows - jnp.mean(rows, axis=-1, keepdims=True)
    scale = lax.rsqrt(jnp.mean(centered * centered, axis=-1, keepdims=True) + norm_eps)
    unit = centered * scale
    inner = gradient * gain
    back = inner - jnp.mean(inner, axis=-1, keepdims=True)
    back = (back - unit * jnp.mean(inner * unit, axis=-1, keepdims=True)) * scale
    gains = jnp.sum(gradient * unit, axis=0, keepdims=True)
    return back, gains, jnp.sum(gradient, axis=0, keepdims=True)


def key_mask(rows, image_rows, valid):
    row = lax.broadcasted_iota(jnp.int32, (rows, rows), 0)
    column = lax.broadcasted_iota(jnp.int32, (rows, rows), 1)
    if rows == image_rows:
        return column < valid
    mask = None
    for start in range(0, rows, image_rows):
        inside = (row >= start) & (row < start + image_rows)
        inside = inside & (column >= start) & (column < start + valid)
        mask = inside if mask is None else mask | inside
    return mask


def head_lanes(rows, head_size):
    lane = lax.broadcasted_iota(jnp.int32, (rows, 128), 1)
    return [
        jnp.where((lane >= start) & (lane < start + head_size), 1.0, 0.0).astype(low)
        for start in range(0, 128, head_size)
    ]


def softmax_rows(queries, key_rows, mask, score_scale):
    scores = product_right(queries, key_rows) * score_scale
    scores = jnp.where(mask, scores, -1e30)
    powers = jnp.exp(scores - jnp.max(scores, axis=-1, keepdims=True))
    return powers * (1.0 / jnp.sum(powers, axis=-1, keepdims=True))


def chunk_of(size):
    return 512 if size % 512 == 0 else 256 if size % 256 == 0 else size


def layer_kernel(
    image_rows, valid, head_size, x, packed_w, out_w, up0, up1, down0, down1, norms,
    result, normed, packed, merged, mixed, second, pre0, pre1, hidden0, hidden1,
):
    rows, width = x.shape
    normed[...] = norm_forward(x[...], norms[0:1, :], norms[1:2, :]).astype(low)

    @pl.loop(0, 3)
    def _(part):
        columns = pl.ds(pl.multiple_of(part * width, 128), width)
        packed[:, columns] = product(normed[...], packed_w[:, columns]).astype(low)

    @pl.loop(0, width // 128)
    def _(group):
        mask = key_mask(rows, image_rows, valid)
        base = group * 128
        queries, key_rows, value_rows = (
            packed[:, pl.ds(pl.multiple_of(part * width + base, 128), 128)] for part in range(3)
        )
        total = jnp.zeros((rows, 128), jnp.float32)
        for lanes in head_lanes(rows, head_size):
            shares = softmax_rows(queries * lanes, key_rows, mask, head_size ** (-0.5))
            total = total + product(shares.astype(low), value_rows * lanes)
        merged[:, pl.ds(pl.multiple_of(base, 128), 128)] = total.astype(low)

    mixed[...] = x[...] + product(merged[...], out_w[...])
    second[...] = norm_forward(mixed[...], norms[2:3, :], norms[3:4, :]).astype(low)
    result[...] = mixed[...]
    for up, down, pre, hidden in ((up0, down0, pre0, hidden0), (up1, down1, pre1, hidden1)):
        size = chunk_of(up.shape[1])

        @pl.loop(0, up.shape[1] // size)
        def _(part):
            columns = pl.ds(pl.multiple_of(part * size, 128), size)
            value = product(second[...], up[:, columns])
            pre[:, columns] = value
            half = 0.5 * (1.0 + lax.erf(value * math.sqrt(0.5)))
            units = (value * half).astype(low)
            hidden[:, columns] = units
            result[...] += product_right(units, down[:, columns])


def feed_kernel(
    gradient, mixed, pre0, pre1, up0, up1, down0, down1, norms,
    grad_mixed, branch, attn, grad_pre0, grad_pre1, norm_grads, total,
):
    branch[...] = gradient[...].astype(low)
    total[...] = jnp.zeros_like(total)
    for up, down, pre, grad_pre in ((up0, down0, pre0, grad_pre0), (up1, down1, pre1, grad_pre1)):
        size = chunk_of(up.shape[1])

        @pl.loop(0, up.shape[1] // size)
        def _(part):
            columns = pl.ds(pl.multiple_of(part * size, 128), size)
            value = pre[:, columns]
            slope = 0.5 * (1.0 + lax.erf(value * math.sqrt(0.5)))
            slope += value * jnp.exp(-0.5 * value * value) * (1.0 / math.sqrt(2.0 * math.pi))
            units = (product(branch[...], down[:, columns]) * slope).astype(low)
            grad_pre[:, columns] = units
            total[...] += product_right(units, up[:, columns])

    back, gains, shifts = norm_backward(mixed[...], norms[2:3, :], total[...])
    back = back + gradient[...]
    grad_mixed[...] = back
    attn[...] = back.astype(low)
    norm_grads[0:1, :] = gains
    norm_grads[1:2, :] = shifts


def attention_kernel(
    image_rows, valid, head_size, grad_mixed, attn, x, packed, packed_w, out_w, norms,
    grad_x, grad_packed, norm_grads, grad_merged,
):
    rows, width = x.shape
    score_scale = head_size ** (-0.5)
    grad_merged[...] = product_right(attn[...], out_w[...]).astype(low)

    @pl.loop(0, width // 128)
    def _(group):
        mask = key_mask(rows, image_rows, valid)
        base = group * 128
        places = [pl.ds(pl.multiple_of(part * width + base, 128), 128) for part in range(3)]
        queries, key_rows, value_rows = (packed[:, place] for place in places)
        grad_out = grad_merged[:, pl.ds(pl.multiple_of(base, 128), 128)]
        totals = [jnp.zeros((rows, 128), jnp.float32)] * 3
        for lanes in head_lanes(rows, head_size):
            own_queries, own_out = queries * lanes, grad_out * lanes
            shares = softmax_rows(own_queries, key_rows, mask, score_scale)
            grad_shares = product_right(own_out, value_rows)
            inner = jnp.sum(shares * grad_shares, axis=-1, keepdims=True)
            grad_scores = (shares * (grad_shares - inner)).astype(low)
            totals = [
                totals[0] + product(grad_scores, key_rows * lanes),
                totals[1] + product_left(grad_scores, own_queries),
                totals[2] + product_left(shares.astype(low), own_out),
            ]
        scales = (score_scale, score_scale, 1.0)
        for place, total, scale in zip(places, totals, scales):
            grad_packed[:, place] = (total * scale).astype(low)

    grad_normed = product_right(grad_packed[...], packed_w[...])
    back, gains, shifts = norm_backward(x[...], norms[0:1, :], grad_normed)
    grad_x[...] = back + grad_mixed[...]
    norm_grads[0:1, :] = gains
    norm_grads[1:2, :] = shifts


def loss_kernel(
    scaling, x, pixels, chosen, pixel_w, norms, final, grad_pred, grad_x, norm_grads, loss
):
    final[...] = norm_forward(x[...], norms[4:5, :], norms[5:6, :]).astype(low)
    errors = product(final[...], pixel_w[...]) - pixels[...].astype(jnp.float32)
    errors = errors * chosen[...]
    loss[...] = jnp.broadcast_to(jnp.sum(errors * errors) * scaling, loss.shape)
    grad_pred[...] = (errors * (2.0 * scaling)).astype(low)
    grad_final = product_right(grad_pred[...], pixel_w[...])
    back, gains, shifts = norm_backward(x[...], norms[4:5, :], grad_final)
    grad_x[...] = back
    norm_grads[0:1, :] = gains
    norm_grads[1:2, :] = shifts


def call_blocks(kernel, block, blocked, whole, outs, scratch=(), flops=0):
    steps = blocked[0].shape[0] // block
    specs = [pl.BlockSpec((block, member.shape[1]), lambda i: (i, 0)) for member in blocked]
    specs += [
        pl.BlockSpec(member.shape, lambda i: (0, 0), pipeline_mode=pl.Buffered(1))
        for member in whole
    ]
    shapes = [jax.ShapeDtypeStruct((rows * steps, columns), kind) for rows, columns, kind in outs]
    size = sum(member.size * member.dtype.itemsize for member in (*blocked, *whole, *shapes))
    return pl.pallas_call(
        kernel,
        grid=(steps,),
        in_specs=specs,
        out_specs=[pl.BlockSpec((rows, columns), lambda i: (i, 0)) for rows, columns, _ in outs],
        out_shape=shapes,
        scratch_shapes=list(scratch),
        compiler_params=pltpu.CompilerParams(vmem_limit_bytes=60 << 20),
        cost_estimate=pl.CostEstimate(flops=flops, bytes_accessed=size, transcendentals=0),
    )(*blocked, *whole)


def layer_forward(stream, packed_w, out_w, feed, norms, head_count, block, image_rows, valid):
    rows, width = stream.shape
    units = feed[0][0].shape[1]
    outs = [
        (block, width, jnp.float32),
        (block, width, low),
        (block, 3 * width, low),
        (block, width, low),
        (block, width, jnp.float32),
        (block, width, low),
        (block, units, jnp.float32),
        (block, units, jnp.float32),
        (block, units, low),
        (block, units, low),
    ]
    return call_blocks(
        partial(layer_kernel, image_rows, valid, width // head_count),
        block,
        [stream],
        [packed_w, out_w, *feed[0], *feed[1], norms],
        outs,
        flops=2 * rows * width * (4 * width + 4 * units + 2 * block),
    )


def feed_backward(gradient, saved, feed, norms, block):
    _, normed, packed, merged, mixed, second, pre0, pre1, hidden0, hidden1 = saved
    rows, width = gradient.shape
    units = pre0.shape[1]
    grad_mixed, branch, attn, grad_pre0, grad_pre1, norm_grads = call_blocks(
        feed_kernel,
        block,
        [gradient, mixed, pre0, pre1],
        [*feed[0], *feed[1], norms],
        [
            (block, width, jnp.float32),
            (block, width, low),
            (block, width, low),
            (block, units, low),
            (block, units, low),
            (8, width, jnp.float32),
        ],
        [pltpu.VMEM((block, width), jnp.float32)],
        flops=8 * rows * width * units,
    )
    grad_down = (product_left(branch, hidden0), product_left(branch, hidden1).astype(low))
    grad_up = (product_left(second, grad_pre0), product_left(second, grad_pre1).astype(low))
    return grad_mixed, attn, grad_down, grad_up, norm_rows(norm_grads)


def attention_backward(
    grad_mixed, attn, stream, saved, packed_w, out_w, norms, head_count, block, image_rows, valid
):
    _, normed, packed, merged, mixed, second, pre0, pre1, hidden0, hidden1 = saved
    rows, width = stream.shape
    grad_x, grad_packed, norm_grads = call_blocks(
        partial(attention_kernel, image_rows, valid, width // head_count),
        block,
        [grad_mixed, attn, stream, packed],
        [packed_w, out_w, norms],
        [(block, width, jnp.float32), (block, 3 * width, low), (8, width, jnp.float32)],
        [pltpu.VMEM((block, width), low)],
        flops=2 * rows * width * (4 * width + 5 * block),
    )
    return grad_x, split_grad(normed, grad_packed), split_grad(merged, attn), norm_rows(norm_grads)


def norm_rows(partial_sums):
    sums = jnp.sum(partial_sums.reshape(-1, 8, partial_sums.shape[1]), axis=0)
    return sums[0], sums[1]


def adam_update(weight, first, second, gradient, rate):
    first = beta_one * first + (1.0 - beta_one) * gradient
    second = beta_two * second + (1.0 - beta_two) * gradient * gradient
    fix_one = 1.0 - beta_one**STEP
    fix_two = 1.0 - beta_two**STEP
    step_dir = first / fix_one / (jnp.sqrt(second / fix_two) + adam_eps)
    return (weight - rate * (step_dir + decay_rate * weight), first, second)


def own_rows(array):
    pieces = lax.axis_size(TENSOR)
    rows = array.shape[0] // pieces
    return lax.dynamic_slice_in_dim(array, lax.axis_index(TENSOR) * rows, rows, 0)


def after(value, *others):
    if not others:
        return value
    zero = sum(other[(0,) * other.ndim].astype(jnp.float32) for other in others) * 0.0
    return value + zero.astype(value.dtype)


class Links:
    def __init__(self):
        self.zero = None

    def swap(self, array, axis, step):
        if self.zero is not None:
            array = array + self.zero.astype(array.dtype)
        return swap(array, axis, step)

    def round(self, *jobs):
        received = []
        for job in jobs:
            known = len(job.received)
            job.go()
            received.extend(job.received[known:])
        corners = [other[(0,) * other.ndim].astype(jnp.float32) for other in received]
        self.zero = sum(corners) * 0.0


class Job:
    def __init__(self, steps):
        self.steps, self.result, self.ended = steps, None, False
        self.received = []

    def go(self, count=1):
        for _ in range(count):
            if self.ended:
                return
            try:
                self.received.append(next(self.steps))
            except StopIteration as stop:
                self.result, self.ended = stop.value, True

    def finish(self):
        while not self.ended:
            self.go()
        return self.result


def swap(array, axis, step):
    size = lax.axis_size(axis)
    return lax.ppermute(array, axis, [(i, i ^ step) for i in range(size)])


def halves(array):
    second = lax.axis_index("core") == 1
    half = array.shape[-1] // 2
    lower, upper = array[:, :half], array[:, half:]
    return jnp.where(second, upper, lower), jnp.where(second, lower, upper)


def join_halves(own, other):
    second = lax.axis_index("core") == 1
    return jnp.concatenate(
        [jnp.where(second, other, own), jnp.where(second, own, other)], axis=-1
    )


def gather_axis(links, array, axis, place):
    size = lax.axis_size(axis)
    step, at = size // 2, place
    while step >= 1:
        array = jnp.expand_dims(array, at)
        other = links.swap(array, axis, step)
        yield other
        upper = (lax.axis_index(axis) // step) % 2 == 1
        array = jnp.concatenate(
            [jnp.where(upper, other, array), jnp.where(upper, array, other)], axis=at
        )
        at += 1
        step //= 2
    return array.reshape(array.shape[:place] + (size,) + array.shape[at:])


def gather_rows(links, piece, shard_first=False):
    columns = piece.shape[1:]
    if shard_first:
        whole = yield from gather_axis(links, piece, "shard", 0)
        whole = yield from gather_axis(links, whole, "heads", 1)
    else:
        whole = yield from gather_axis(links, piece, "heads", 0)
        whole = yield from gather_axis(links, whole, "shard", 0)
    return whole.reshape((-1,) + columns)


def gather_mats(links, matrices):
    send = jnp.concatenate([halves(member)[0] for member in matrices], axis=1).astype(low)
    own = yield from gather_rows(links, send)
    other = links.swap(own, "core", 1)
    yield other
    results, at = [], 0
    for member in matrices:
        until = at + member.shape[1] // 2
        results.append(join_halves(own[:, at:until], other[:, at:until]))
        at = until
    return results


def gather_feed(links, piece, shard_first):
    whole = yield from gather_rows(links, piece, shard_first)
    step = 1
    while step < lax.axis_size("pair"):
        other = links.swap(whole, "pair", step)
        yield other
        whole = jnp.concatenate([whole, other], axis=1)
        step *= 2
    other = links.swap(whole, "core", 1)
    yield other
    return [whole, other]


def reduce_axis(links, arrays, axis, place):
    size = lax.axis_size(axis)
    bits = size.bit_length() - 1
    mine = lax.axis_index(axis)
    arrays = [
        member.reshape(member.shape[:place] + (2,) * bits + member.shape[place + 1 :])
        for member in arrays
    ]
    for bit in range(bits):
        pick = partial(lax.dynamic_index_in_dim, axis=place + bits - 1 - bit, keepdims=False)
        upper = (mine >> bit) % 2
        send = [pick(member, 1 - upper).astype(low) for member in arrays]
        send = jnp.concatenate(send, axis=-1) if len(send) > 1 else send[0]
        keep = [pick(member, upper) for member in arrays]
        keep = jnp.concatenate(keep, axis=-1) if len(keep) > 1 else keep[0]
        other = links.swap(send, axis, 1 << bit)
        yield other
        arrays = [keep + other.astype(jnp.float32)]
    return arrays[0]


def split_grad(left, right):
    own, other = halves(right)
    return product_left(left, own), product_left(left, other).astype(low)


def scatter_mats(links, pairs, shard_first):
    shard, heads = (lax.axis_size(axis) for axis in AXES[:2])
    others = [links.swap(send, "core", 1) for _, send in pairs]
    yield sum(other[:8, :128] for other in others)
    sums = [
        (own + other.astype(jnp.float32)).reshape(shard, heads, -1, own.shape[1])
        for (own, _), other in zip(pairs, others)
    ]
    if shard_first:
        total = yield from reduce_axis(links, sums, "shard", 0)
        total = yield from reduce_axis(links, [total], "heads", 0)
    else:
        total = yield from reduce_axis(links, sums, "heads", 1)
        total = yield from reduce_axis(links, [total], "shard", 0)
    step = 1
    while step < lax.axis_size("pair"):
        total = total.astype(low)
        other = links.swap(total, "pair", step)
        yield other
        total = total.astype(jnp.float32) + other.astype(jnp.float32)
        step *= 2
    return total


def scatter_feed(links, own, send):
    shard, heads, pair = (lax.axis_size(axis) for axis in AXES[:3])
    other = links.swap(send, "core", 1)
    yield other
    total = own + other.astype(jnp.float32)
    step = pair // 2
    while step >= 1:
        half = total.shape[1] // 2
        other = links.swap(total[:, half:].astype(low), "pair", step)
        yield other
        total = total[:, :half] + other.astype(jnp.float32)
        step //= 2
    total = total.reshape(shard, heads, -1, total.shape[1])
    total = yield from reduce_axis(links, [total], "shard", 0)
    return (yield from reduce_axis(links, [total], "heads", 0))


def butterfly_sum(values):
    for axis in AXES[::-1]:
        step = 1
        while step < lax.axis_size(axis):
            values = values + swap(values, axis, step)
            step *= 2
    return values


def per_device(
    patch_pixels,
    keep_index,
    restore_index,
    masked,
    encoder_mats,
    encoder_mats_first,
    encoder_mats_second,
    decoder_mats,
    decoder_mats_first,
    decoder_mats_second,
    encoder_feed,
    encoder_feed_first,
    encoder_feed_second,
    decoder_feed,
    decoder_feed_first,
    decoder_feed_second,
    encoder_norms,
    encoder_norms_first,
    encoder_norms_second,
    decoder_norms,
    decoder_norms_first,
    decoder_norms_second,
):
    masters = (encoder_mats, decoder_mats, encoder_feed, decoder_feed, encoder_norms, decoder_norms)
    firsts = (
        encoder_mats_first,
        decoder_mats_first,
        encoder_feed_first,
        decoder_feed_first,
        encoder_norms_first,
        decoder_norms_first,
    )
    seconds = (
        encoder_mats_second,
        decoder_mats_second,
        encoder_feed_second,
        decoder_feed_second,
        encoder_norms_second,
        decoder_norms_second,
    )
    rates = (learn_rate, learn_rate, learn_rate, learn_rate, norm_rate, norm_rate)
    groups = lax.axis_size("shard") * lax.axis_size("heads")
    pieces = lax.axis_size(TENSOR)
    devices = groups * pieces

    patch_pixels = own_rows(patch_pixels)
    keep_index = own_rows(keep_index)
    restore_index = own_rows(restore_index)
    masked = own_rows(masked)
    images, patches, pixel_dim = patch_pixels.shape
    kept = keep_index.shape[1]

    enc_rows, enc_cols = encoder_mats.shape
    dec_rows, dec_cols = decoder_mats.shape
    width_enc = enc_rows * groups
    width_dec = dec_rows * groups
    enc_size, dec_size = encoder_norms.size, decoder_norms.size
    tables = jnp.concatenate([encoder_norms.reshape(-1), decoder_norms.reshape(-1)])
    tables = jnp.pad(tables, (0, -tables.size % 1024)).reshape(1, -1, 128).astype(low)
    links = Links()
    tables = Job(gather_rows(Links(), tables)).finish().reshape(groups, -1)
    enc_norm = tables[:, :enc_size].reshape(groups, -1, enc_rows).transpose(1, 0, 2)
    enc_norm = enc_norm.reshape(-1, width_enc).astype(jnp.float32)
    dec_norm = tables[:, enc_size : enc_size + dec_size].reshape(groups, -1, dec_rows)
    dec_norm = dec_norm.transpose(1, 0, 2).reshape(-1, width_dec).astype(jnp.float32)

    enc_cuts = (0, width_enc, 4 * width_enc, 5 * width_enc, enc_cols)
    dec_cuts = (0, 3 * width_dec, 4 * width_dec, dec_cols)
    enc_parts = [encoder_mats[:, a:b] for a, b in zip(enc_cuts, enc_cuts[1:])]
    dec_parts = [decoder_mats[:, a:b] for a, b in zip(dec_cuts, dec_cuts[1:])]
    enc_up, enc_down = encoder_feed.astype(low)
    dec_up, dec_down = decoder_feed.astype(low)
    eh = Job(gather_mats(links, enc_parts[:2]))
    et = Job(gather_mats(links, enc_parts[2:]))
    eu = Job(gather_feed(links, enc_up, False))
    ed = Job(gather_feed(links, enc_down, True))
    dm = Job(gather_mats(links, dec_parts))
    du = Job(gather_feed(links, dec_up, False))
    dd = Job(gather_feed(links, dec_down, True))
    for job in (eh, ed, et, dd, eh, ed, et, eu, eh, ed, eu, et, dd, eu, ed, dm, dd, eu):
        job.go()
    for job in (dm, du, dd, dm, du, du, du):
        job.go()
    emb_w, enc_packed = eh.finish()
    enc_out, proj_w = et.finish()
    enc_feed = [eu.finish(), ed.finish()]
    dec_packed, dec_out, pixel_w = dm.finish()
    dec_feed = [du.finish(), dd.finish()]

    enc_pad = -(-kept // 64) * 64
    dec_pad = -(-patches // 16) * 16
    keep_pad = jnp.pad(keep_index, ((0, 0), (0, enc_pad - kept)), constant_values=-1)
    spots = jnp.arange(patches, dtype=jnp.int32)
    picks = (keep_pad[:, :, None] == spots).astype(low)
    picked = jnp.einsum("bkp,bpd->bkd", picks, patch_pixels, preferred_element_type=jnp.float32)
    picked = picked.astype(low).reshape(images * enc_pad, pixel_dim)
    places = jnp.asarray(positions(patches, width_enc))[jnp.maximum(keep_pad, 0)]
    enc_stream = product(picked, emb_w) + places.reshape(images * enc_pad, width_enc)
    enc_block = images * enc_pad
    enc_shape = (enc_block, enc_pad, kept)
    enc_saved = layer_forward(
        enc_stream, enc_packed, enc_out, enc_feed, enc_norm, HEADS_E, *enc_shape
    )
    enc_flat = enc_saved[0]
    enc_final = layer_norm(enc_flat, enc_norm[4], enc_norm[5]).astype(low)
    latent = product(enc_final, proj_w).reshape(images, enc_pad, width_dec)
    restore_pad = jnp.pad(
        restore_index, ((0, 0), (0, dec_pad - patches)), constant_values=enc_pad + patches
    )
    slots = jnp.arange(enc_pad, dtype=jnp.int32)
    seen = restore_pad[:, :, None] < kept
    routes = ((restore_pad[:, :, None] == slots) & seen).astype(jnp.float32)
    table = jnp.pad(positions(patches, width_dec), ((0, dec_pad - patches), (0, 0)))
    dec_stream = jnp.einsum("bpk,bkd->bpd", routes, latent, precision=lax.Precision.HIGHEST)
    dec_stream = dec_stream + jnp.where(seen, 0.0, dec_norm[6]) + table
    dec_stream = dec_stream.reshape(images * dec_pad, width_dec)
    dec_shape = (dec_pad, dec_pad, patches)
    dec_saved = layer_forward(
        dec_stream, dec_packed, dec_out, dec_feed, dec_norm, HEADS_D, *dec_shape
    )
    row_pad = ((0, 0), (0, dec_pad - patches))
    pixels = jnp.pad(patch_pixels, (*row_pad, (0, 0))).reshape(images * dec_pad, pixel_dim)
    chosen = jnp.pad(masked.astype(jnp.float32), row_pad)
    scaling = 1.0 / (images * devices * (patches - kept) * pixel_dim)
    dec_final, grad_pred, grad_stream, dec_third, losses = call_blocks(
        partial(loss_kernel, scaling),
        dec_pad,
        [dec_saved[0], pixels, chosen.reshape(images * dec_pad, 1)],
        [pixel_w, dec_norm],
        [
            (dec_pad, width_dec, low),
            (dec_pad, pixel_dim, low),
            (dec_pad, width_dec, jnp.float32),
            (8, width_dec, jnp.float32),
            (8, 128, jnp.float32),
        ],
        flops=4 * images * dec_pad * width_dec * pixel_dim,
    )
    dec_third = norm_rows(dec_third)
    loss_local = jnp.sum(losses.reshape(images, 8, 128)[:, 0, 0])
    grad_pixel_w = split_grad(dec_final, grad_pred)
    grad_mixed, attn, grad_down, grad_up, dec_second = feed_backward(
        grad_stream, dec_saved, dec_feed, dec_norm, dec_pad
    )
    dd = Job(scatter_feed(links, *grad_down))
    du = Job(scatter_feed(links, *grad_up))
    for job in (dd, du):
        job.go()
    grad_stream, grad_packed_w, grad_out_w, dec_first = attention_backward(
        grad_mixed, attn, dec_stream, dec_saved, dec_packed, dec_out, dec_norm, HEADS_D, *dec_shape
    )
    dm = Job(scatter_mats(links, [grad_packed_w, grad_out_w, grad_pixel_w], False))
    dm.go()

    grad_cube = grad_stream.reshape(images, dec_pad, width_dec)
    grad_latent = jnp.einsum(
        "bpk,bpd->bkd", routes, grad_cube, precision=lax.Precision.HIGHEST
    ).reshape(images * enc_pad, width_dec)
    grad_latent = grad_latent.astype(low)
    grad_mask = jnp.sum(jnp.where(seen, 0.0, grad_cube), axis=(0, 1))
    grad_proj = split_grad(enc_final, grad_latent)
    grad_final = product_right(grad_latent, proj_w)
    final_pull = jax.vjp(layer_norm, enc_flat, enc_norm[4], enc_norm[5])[1]
    grad_stream, *enc_third = final_pull(grad_final)
    grad_mixed, attn, grad_down, grad_up, enc_second = feed_backward(
        grad_stream, enc_saved, enc_feed, enc_norm, enc_block
    )
    ed = Job(scatter_feed(links, *grad_down))
    eu = Job(scatter_feed(links, *grad_up))
    for job in (ed, eu):
        job.go()
    grad_stream, grad_packed_w, grad_out_w, enc_first = attention_backward(
        grad_mixed, attn, enc_stream, enc_saved, enc_packed, enc_out, enc_norm, HEADS_E, *enc_shape
    )
    grad_embed = split_grad(picked, grad_stream.astype(low))
    et = Job(scatter_mats(links, [grad_out_w, grad_proj], True))
    eh = Job(scatter_mats(links, [grad_embed, grad_packed_w], True))
    for job in (eh, et):
        job.go()
    ed.go()
    links.zero = ed.received[0][0, 0].astype(jnp.float32) * 0.0
    links.round(eh, dm)
    links.zero = links.zero + ed.received[1][0, 0].astype(jnp.float32) * 0.0
    links.round(eu, ed, et, dm, eh)
    links.round(dd, du, eu, dm, eh, et, ed)
    links.round(eh, dm, dd, du, eu, et, ed)
    links.zero = None
    dec_feed_sum = (du.finish(), dd.finish())
    dec_mats_sum = dm.finish()
    enc_tail_sum = et.finish()
    enc_feed_sum = (eu.finish(), ed.finish())
    enc_head_sum = eh.finish()

    norm_grads = [
        jnp.stack([*enc_first, *enc_second, *enc_third]),
        jnp.stack([*dec_first, *dec_second, *dec_third, grad_mask]),
    ]
    copies = lax.axis_size("pair")
    squares = sum(jnp.sum(jnp.square(member)) for member in (*enc_feed_sum, *dec_feed_sum))
    squares += sum(
        jnp.sum(jnp.square(member)) for member in (enc_tail_sum, enc_head_sum, dec_mats_sum)
    ) * (1.0 / copies)
    packed = jnp.concatenate(
        [member.reshape(-1) for member in norm_grads] + [jnp.stack([loss_local, squares])]
    )
    packed = jnp.pad(packed, (0, -packed.size % 1024)).reshape(-1, 128)
    packed = butterfly_sum(packed).reshape(-1)
    enc_total, dec_total = (member.size for member in norm_grads)
    both_total = enc_total + dec_total
    loss = packed[both_total]
    total = packed[both_total + 1] + jnp.sum(jnp.square(packed[:both_total]))
    group = lax.axis_index(("shard", "heads"))
    enc_norm_sum = packed[:enc_total].reshape(-1, groups, enc_rows)
    dec_norm_sum = packed[enc_total : enc_total + dec_total].reshape(-1, groups, dec_rows)
    enc_norm_sum = lax.dynamic_index_in_dim(enc_norm_sum, group, 1, keepdims=False)
    dec_norm_sum = lax.dynamic_index_in_dim(dec_norm_sum, group, 1, keepdims=False)

    def whole_columns(own, parts):
        other = swap(own, "core", 1)
        results, at = [], 0
        for member in parts:
            until = at + member.shape[1] // 2
            results.append(join_halves(own[:, at:until], other[:, at:until]))
            at = until
        return results

    reduced = (
        jnp.concatenate(
            whole_columns(enc_head_sum, enc_parts[:2]) + whole_columns(enc_tail_sum, enc_parts[2:]),
            axis=1,
        ),
        jnp.concatenate(whole_columns(dec_mats_sum, dec_parts), axis=1),
        jnp.stack(enc_feed_sum),
        jnp.stack(dec_feed_sum),
        enc_norm_sum,
        dec_norm_sum,
    )
    norm = jnp.sqrt(total)
    factor = clip_limit / jnp.maximum(norm, clip_limit)
    results = [loss, norm]
    for weight, first, second, gradient, rate in zip(masters, firsts, seconds, reduced, rates):
        results.extend(adam_update(weight, first, second, gradient * factor, rate))
    return tuple(results)


def solution(mesh):
    shard, heads, tensor = (mesh.shape[axis] for axis in ("shard", "heads", "tensor"))
    mesh = Mesh(mesh.devices.reshape(shard, heads, tensor // 2, 2), AXES)
    rows = P(("shard", "heads"), None)
    feeds = P(None, ("shard", "heads"), TENSOR)
    norms = P(None, ("shard", "heads"))
    states = (rows,) * 6 + (feeds,) * 6 + (norms,) * 6
    return jax.shard_map(
        per_device,
        mesh=mesh,
        in_specs=(P(("shard", "heads"), None, None), rows, rows, rows) + states,
        out_specs=(P(), P()) + states,
        check_vma=False,
    )
```
